32 devices in a mesh: seq: 8 (over z, y), tp: 4 (over x, core).
Axes of the slice: x: 2, y: 2, z: 4, core: 2. Of those that a mesh axis runs over, the one named last changes fastest.
Arguments:
- tokens: bfloat16 [4, 2048, 1024], P('tp', 'seq'), may hold values from -6 to 6
- lengths: int32 [4], replicated, may hold values from 256 to 2048, as said below
- forget: float32 [8], replicated, as said below
- w_mix: bfloat16 [1024, 4096], replicated, may hold values from -0.1875 to 0.1875
- w_out: bfloat16 [1024, 1024], replicated, may hold values from -0.1875 to 0.1875
- w_gate: bfloat16 [1024, 2816], P(None, 'tp'), may hold values from -0.1875 to 0.1875
- w_up: bfloat16 [1024, 2816], P(None, 'tp'), may hold values from -0.1875 to 0.1875
- w_down: bfloat16 [1024, 2816], P(None, 'tp'), may hold values from -0.109375 to 0.109375
- cotangent: bfloat16 [4, 2048, 1024], P('tp', 'seq'), may hold values from -6 to 6
Outputs:
- out: bfloat16 [4, 2048, 1024], P('tp', 'seq')
- d_tokens: bfloat16 [4, 2048, 1024], P('tp', 'seq')
- d_mix: float32 [1024, 4096], P('seq')
- d_out: float32 [1024, 1024], P('seq')
- d_gate: float32 [1024, 2816], P('seq', 'tp')
- d_up: float32 [1024, 2816], P('seq', 'tp')
- d_down: float32 [1024, 2816], P('seq', 'tp')
The draws below stay inside these ranges and needn't reach their ends.
Inputs may be any that keep to these rules, and one draw needn't show every extreme that they name: Positions at and after lengths[i] of sequence i are padding; in every draw one sequence has all 2048 positions. A head's state is multiplied by exp(-forget) for every position that it moves on.
All inputs are finite; a program needn't handle non-finite values.
Results may differ from the reference program's by a relative error of at most 0.02.
Values may be sent and summed in bfloat16 or wider, within the bound.
No kernel may reach another device: no remote copies, remote signals or barrier semaphores. Data moves between devices by JAX's collectives and lax.ppermute only.
A program may use at most 384 MiB of HBM per device.

```python
import math
import jax
import jax.numpy as jnp
import numpy as np
from jax import lax

D = 1024
HEADS = 8
HEAD = 128
FF = 2816
ITEMS = 4
MAXLEN = 2048


def draw_lengths(key, part):
    first, second = jax.random.split(key)
    spans = jax.random.randint(first, (ITEMS,), MAXLEN // 8, MAXLEN + 1)
    longest = jax.random.randint(second, (), 0, ITEMS)
    return jnp.where(jnp.arange(ITEMS) == longest, MAXLEN, spans).astype(jnp.int32)


def draw_forget(key, part):
    order_key, fast_key, slow_key = jax.random.split(key, 3)
    order = jax.random.permutation(order_key, HEADS)
    fast = jnp.exp(jax.random.uniform(fast_key, (HEADS,), jnp.float32, math.log(1.0 / 50.0), math.log(1.0 / 30.0)))
    slow = jnp.exp(jax.random.uniform(slow_key, (HEADS,), jnp.float32, math.log(0.1 / MAXLEN), math.log(2.0 / MAXLEN)))
    fast_heads = HEADS // 2
    return jnp.where(order < fast_heads, fast, slow).astype(jnp.float32)


def block_levels(key, shape, cuts, low, largest):
    level, own = 1.0, jax.random.fold_in(key, 6)
    for dim, blocks in cuts:
        heights = jnp.exp(jax.random.uniform(jax.random.fold_in(own, dim), (blocks,), jnp.float32, low / len(cuts), largest / len(cuts)))
        level = level * jnp.repeat(heights, shape[dim] // blocks).reshape([-1 if axis == dim else 1 for axis in range(len(shape))])
    return level


def noise(rng, dims, deviation, most, cuts=(), held_as=jnp.bfloat16):
    factor_of = block_levels(rng, dims, cuts, -0.22, 0.18) if cuts else 1.0
    entries = jax.random.normal(rng, dims, jnp.float32) * deviation * factor_of
    return jnp.minimum(jnp.maximum(entries, -most), most).astype(held_as)


def setup_inputs(seed: int = 0) -> dict:
    keys = jax.random.split(jax.random.key(seed), 10)
    return {
        "tokens": noise(keys[0], (ITEMS, MAXLEN, D), 1.0, 6.0, ((0, 4), (1, 8))),
        "lengths": draw_lengths(jax.random.fold_in(keys[9], 71), 0),
        "forget": draw_forget(jax.random.fold_in(keys[9], 71), 0),
        "w_mix": noise(keys[3], (D, 4 * D), D ** -0.5, 0.1875),
        "w_out": noise(keys[4], (D, D), D ** -0.5, 0.1875),
        "w_gate": noise(keys[5], (D, FF), D ** -0.5, 0.1875, ((1, 4),)),
        "w_up": noise(keys[6], (D, FF), D ** -0.5, 0.1875, ((1, 4),)),
        "w_down": noise(keys[7], (D, FF), FF ** -0.5, 0.109375, ((1, 4),)),
        "cotangent": noise(keys[8], (ITEMS, MAXLEN, D), 1.0, 6.0, ((0, 4), (1, 8))),
    }


@jax.custom_vjp
def low(v):
    return lax.optimization_barrier(v.astype(jnp.bfloat16)).astype(jnp.float32)

@jax.custom_vjp
def low_back(v):
    return v

def low_keep(v):
    return (low(v), None)

def low_pass(kept, grad):
    return (grad,)

def back_keep(v):
    return (v, None)

def back_low(kept, grad):
    return (low(grad),)
low.defvjp(low_keep, low_pass)
low_back.defvjp(back_keep, back_low)
EPSILON = 1e-06

def simple_norm(value):
    return value * lax.rsqrt(lax.optimization_barrier(jnp.mean(value * value, axis=-1, keepdims=True)) + EPSILON)

def contract(form, left, right):
    return jnp.einsum(form, left, right, precision=lax.Precision.HIGHEST, preferred_element_type=jnp.float32)

def matmul(left, right):
    return jnp.dot(left, right, precision=lax.Precision.HIGHEST)

def rotation(places, width):
    table = np.floor(65536.0 / (2.0 * math.pi) * 10000.0 ** (-np.arange(width) / width) + 0.5).astype(np.int32)
    phase = jnp.remainder(places[:, None] * jnp.asarray(table)[None, :], 65536)
    angle = phase.astype(jnp.float32) * (2.0 * math.pi / 65536.0)
    return (jnp.cos(angle), jnp.sin(angle))

def rotate_both(raw_query, raw_key, cosine, sine):

    def turn(values):
        values = jax.nn.silu(values)
        return jnp.concatenate([values * cosine[:, None, :], values * sine[:, None, :]], axis=-1)
    return (turn(raw_query), turn(raw_key))

def linear_attention(query, key, value, rates):
    length = query.shape[0]
    block = math.gcd(length, 256)
    count = length // block
    ahead = jnp.arange(block, dtype=jnp.int32)
    offsets = ahead.astype(jnp.float32)
    gap = ahead[:, None] - ahead[None, :]
    grid = jnp.where(gap[None] >= 0, jnp.exp(-rates[:, None, None] * jnp.maximum(gap, 0)[None].astype(jnp.float32)), 0.0)
    lead = jnp.exp(-rates[None, :] * (offsets + 1.0)[:, None])
    tail = jnp.exp(-rates[None, :] * (block - 1.0 - offsets)[:, None])
    carried = jnp.exp(-rates * block)

    def advance(state, pieces):
        query_block, key_block, value_block = pieces
        raw_scores = low_back(contract('thc,shc->hts', query_block, key_block))
        scores = low(raw_scores * grid)
        intra = contract('hts,she->the', scores, value_block)
        inter = contract('thc,hce->the', query_block, state) * lead[:, :, None]
        local_state = contract('shc,she->hce', key_block * tail[:, :, None], value_block)
        return (state * carried[:, None, None] + local_state, intra + inter)

    def blocks(values):
        return values.reshape(count, block, values.shape[1], values.shape[2])
    start = jnp.zeros((query.shape[1], query.shape[2], value.shape[2]), jnp.float32)
    final, results = lax.scan(jax.checkpoint(advance), start, (blocks(query), blocks(key), blocks(value)))
    return low_back(results.reshape(length, value.shape[1], value.shape[2]))

def layer(inputs, valid, rates, w_mix, w_out, w_gate, w_up, w_down):
    length = inputs.shape[0]
    normed = low(simple_norm(inputs))
    mixed = low_back(matmul(normed, w_mix))
    raw_query, raw_key, value_raw, update = jnp.split(mixed, 4, axis=1)
    cosine, sine = rotation(jnp.arange(length, dtype=jnp.int32), HEAD)
    query, key = rotate_both(raw_query.reshape(length, HEADS, HEAD), raw_key.reshape(length, HEADS, HEAD), cosine, sine)
    value = low(value_raw.reshape(length, HEADS, HEAD))
    attention = linear_attention(low(query), low(key), value, rates).reshape(length, D)
    gated = low(simple_norm(attention) * update)
    resid = inputs + low_back(matmul(gated, w_out))
    ffn_in = low(simple_norm(resid))
    gate_pre = low_back(matmul(ffn_in, w_gate))
    up_pre = low_back(matmul(ffn_in, w_up))
    hidden = low(gate_pre * up_pre)
    down = low_back(matmul(hidden, w_down.T))
    return jnp.where(valid[:, None], resid + down, 0.0)

def reference(tokens, lengths, forget, w_mix, w_out, w_gate, w_up, w_down, cotangent):
    weights = (w_mix.astype(jnp.float32), w_out.astype(jnp.float32), w_gate.astype(jnp.float32), w_up.astype(jnp.float32), w_down.astype(jnp.float32))
    places = jnp.arange(MAXLEN, dtype=jnp.int32)

    def per_item(totals, pieces):
        item_tokens, item_length, item_cotangent = pieces
        valid = places < item_length

        def forward(inputs, mix_matrix, out_matrix, gate_matrix, up_matrix, down_matrix):
            return layer(inputs, valid, forget, mix_matrix, out_matrix, gate_matrix, up_matrix, down_matrix)
        result, pullback = jax.vjp(forward, item_tokens.astype(jnp.float32), weights[0], weights[1], weights[2], weights[3], weights[4])
        grads = pullback(item_cotangent.astype(jnp.float32))
        totals = tuple((total + grad for total, grad in zip(totals, grads[1:])))
        return (totals, (result.astype(jnp.bfloat16), grads[0].astype(jnp.bfloat16)))
    start = tuple((jnp.zeros_like(matrix) for matrix in weights))
    totals, outputs = lax.scan(per_item, start, (tokens, lengths, cotangent))
    return (outputs[0], outputs[1], totals[0], totals[1], totals[2], totals[3], totals[4])
```

```python
from functools import partial
import math

import jax
import jax.numpy as jnp
import numpy as np
from jax import lax
from jax.sharding import PartitionSpec as P

HEADS = 8
HEAD = 128
EPSILON = 1e-06
BF = jnp.bfloat16
F32 = jnp.float32


def simple_norm(value):
    return value * lax.rsqrt(jnp.mean(value * value, axis=-1, keepdims=True) + EPSILON)


def norm_back(value, upstream):
    r = lax.rsqrt(jnp.mean(value * value, axis=-1, keepdims=True) + EPSILON)
    return r * upstream - value * (r * r * r * jnp.mean(value * upstream, axis=-1, keepdims=True))


def product(form, left, right):
    return jnp.einsum(form, left, right, preferred_element_type=F32)


def dot_tn(left, right, kind=BF):
    return lax.dot_general(left, right, (((0,), (0,)), ((), ())), preferred_element_type=F32).astype(kind)


def dot_nt(left, right):
    return lax.dot_general(left, right, (((1,), (1,)), ((), ())), preferred_element_type=F32)


def rotation(places, width):
    table = np.floor(
        65536.0 / (2.0 * math.pi) * 10000.0 ** (-np.arange(width) / width) + 0.5
    ).astype(np.int32)
    phase = jnp.remainder(places[:, None] * jnp.asarray(table)[None, :], 65536)
    angle = phase.astype(F32) * (2.0 * math.pi / 65536.0)
    return (jnp.cos(angle), jnp.sin(angle))


def swap(array, axis, bit):
    count = lax.axis_size(axis)
    return lax.ppermute(array, axis, [(i, i ^ bit) for i in range(count)])


def shift(array, axis, hop):
    count = lax.axis_size(axis)
    pairs = [(i, i + hop) for i in range(count) if 0 <= i + hop < count]
    return lax.ppermute(array, axis, pairs)


def gather_tp(array):
    near = swap(array, "tp", 1)
    far = swap(array, "tp", 2)
    return [array, near, far, swap(far, "tp", 1)]


def scatter_tp(parts):
    p0, p1, p2, p3 = parts
    r1, r3 = swap(jnp.stack([p1, p3]), "tp", 1)
    far = swap((p2.astype(F32) + r3.astype(F32)).astype(BF), "tp", 2)
    return p0.astype(F32) + r1.astype(F32) + far.astype(F32)


def exchange_tp(pieces, owner):
    mine = lax.dynamic_index_in_dim(pieces, owner, 0, False)
    out = [mine]
    for bit in (1, 2, 3):
        out.append(swap(lax.dynamic_index_in_dim(pieces, owner ^ bit, 0, False), "tp", bit))
    return out


def collect_tp(array, owner):
    parts = gather_tp(array)
    return [lax.select_n(owner, *[parts[j ^ k] for k in range(4)]) for j in range(4)]


def reduce_seq(array):
    count = lax.axis_size("seq")
    if count != 8:
        return lax.psum_scatter(array, "seq", scatter_dimension=0, tiled=True).astype(F32)
    place = lax.axis_index("seq")
    side = place % 2
    layer = place // 2
    rows, columns = array.shape
    blocks = array.reshape(count // 2, 2, rows // count, columns)
    keep = lax.dynamic_index_in_dim(blocks, side, 1, False)
    send = lax.dynamic_index_in_dim(blocks, 1 - side, 1, False)
    total = keep.astype(F32) + swap(send, "seq", 1).astype(F32)
    low = total.astype(BF)
    result = lax.dynamic_index_in_dim(total, layer, 0, False)
    for bit in (1, 2, 3):
        part = lax.dynamic_index_in_dim(low, layer ^ bit, 0, False)
        result = result + swap(part, "seq", 2 * bit).astype(F32)
    return result


def entering_any(state, carried, backward):
    count = lax.axis_size("seq")
    place = lax.axis_index("seq")
    ahead = count - 1 - place if backward else place
    gathered = lax.all_gather(state.astype(BF), "seq")

    def one(hop, total):
        source = count - 1 - hop if backward else hop
        part = lax.dynamic_index_in_dim(gathered, source, 0, False).astype(F32)
        return total * carried[:, None, None] + part

    return lax.fori_loop(0, ahead, one, jnp.zeros(state.shape, F32)).astype(BF)


def entering(state, carried, backward):
    count = lax.axis_size("seq")
    if count != 8:
        return entering_any(state, carried, backward)
    place = lax.axis_index("seq")
    side = place % 2
    half = HEADS // 2
    first = side == (1 if backward else 0)
    hop = -2 if backward else 2
    low = state.astype(BF)
    keep = lax.dynamic_slice_in_dim(low, side * half, half).astype(F32)
    send = lax.dynamic_slice_in_dim(low, (1 - side) * half, half)
    other = swap(send, "seq", 1).astype(F32)
    rate = lax.dynamic_slice_in_dim(carried, side * half, half)[:, None, None]
    pair = jnp.where(first, keep * rate + other, other * rate + keep)
    near = shift(pair.astype(BF), "seq", hop).astype(F32)
    far = shift((pair + rate * rate * near).astype(BF), "seq", 2 * hop).astype(F32)
    before = near + rate * rate * far
    mine = jnp.where(first, before, before * rate + other).astype(BF)
    theirs = swap(jnp.where(first, before * rate + keep, before).astype(BF), "seq", 1)
    return jnp.where(side == 0, jnp.concatenate([mine, theirs]), jnp.concatenate([theirs, mine]))


def on_device(tokens, lengths, forget, w_mix, w_out, w_gate, w_up, w_down, cotangent):
    items, span, width = tokens.shape
    heads = HEADS
    head = HEAD
    place = lax.axis_index("seq")
    owner = lax.axis_index("tp")
    length = lax.dynamic_index_in_dim(lengths, owner, 0, False)
    ahead = jnp.arange(span, dtype=jnp.int32)
    places = place * span + ahead
    valid = (places < length)[:, None]
    offsets = ahead.astype(F32)
    gap = ahead[:, None] - ahead[None, :]
    grid = jnp.where(
        gap[None] >= 0,
        jnp.exp(-forget[:, None, None] * jnp.maximum(gap, 0)[None].astype(F32)),
        0.0,
    )
    lead = jnp.exp(-forget[None, :] * (offsets + 1.0)[:, None])[:, :, None]
    tail = jnp.exp(-forget[None, :] * (span - 1.0 - offsets)[:, None])[:, :, None]
    first = jnp.exp(-forget[None, :] * offsets[:, None])[:, :, None]
    rear = jnp.exp(-forget[None, :] * (span - offsets)[:, None])[:, :, None]
    carried = jnp.exp(-forget * span)
    cosine, sine = rotation(places, head)
    cosine, sine = cosine[:, None, :], sine[:, None, :]
    inputs = tokens.reshape(span, width).astype(F32)
    normed = simple_norm(inputs).astype(BF)

    def turn(values):
        values = jax.nn.silu(values)
        return jnp.concatenate([values * cosine, values * sine], axis=-1).astype(BF)

    def turn_back(raw, grad):
        gate = jax.nn.sigmoid(raw)
        slope = gate * (1.0 + raw * (1.0 - gate))
        return (slope * (grad[:, :, :head] * cosine + grad[:, :, head:] * sine)).reshape(span, width)

    key_value = jnp.dot(normed, w_mix[:, width : 3 * width], preferred_element_type=F32)
    raw_key = key_value[:, :width].reshape(span, heads, head)
    value = key_value[:, width:].reshape(span, heads, head).astype(BF)
    key = turn(raw_key)
    local_state = product("bhc,bhe->hce", key, (value * tail).astype(BF))
    incoming = entering(local_state, carried, False)

    raw_query = jnp.dot(normed, w_mix[:, :width], preferred_element_type=F32).reshape(span, heads, head)
    update = jnp.dot(normed, w_mix[:, 3 * width :], preferred_element_type=F32)
    query = turn(raw_query)
    scores = (product("thc,shc->hts", query, key) * grid).astype(BF)
    intra = product("hts,she->the", scores, value)
    grad_out = jnp.where(valid, cotangent.reshape(span, width).astype(F32), 0.0)
    down_grad = jnp.concatenate(gather_tp(grad_out.astype(BF)))
    hidden_grad = jnp.dot(down_grad, w_down, preferred_element_type=F32)
    normed_all = jnp.concatenate(gather_tp(normed))

    inter = product("thc,hce->the", query, incoming) * lead
    attention = (intra + inter).reshape(span, width)
    attention_normed = simple_norm(attention)
    gated = (attention_normed * update).astype(BF)
    resid = inputs + jnp.dot(gated, w_out, preferred_element_type=F32)
    ffn_in = simple_norm(resid).astype(BF)
    ffn_rows = jnp.concatenate(gather_tp(ffn_in))
    gated_all = jnp.concatenate(gather_tp(gated))

    gate_pre = jnp.dot(ffn_rows, w_gate, preferred_element_type=F32)
    up_pre = jnp.dot(ffn_rows, w_up, preferred_element_type=F32)
    hidden = (gate_pre * up_pre).astype(BF)
    gate_grad = (hidden_grad * up_pre).astype(BF)
    up_grad = (hidden_grad * gate_pre).astype(BF)
    rows_grad = (dot_nt(gate_grad, w_gate) + dot_nt(up_grad, w_up)).astype(BF)
    ffn_grad = scatter_tp(list(rows_grad.reshape(4, span, width)))
    down_terms = dot_nt(hidden, w_down).astype(BF)
    down = scatter_tp(list(down_terms.reshape(4, span, width)))
    out = jnp.where(valid, resid + down, 0.0).astype(BF)

    resid_grad = grad_out + norm_back(resid, ffn_grad)
    mix_grad = resid_grad.astype(BF)
    gated_grad = dot_nt(mix_grad, w_out)
    update_grad = gated_grad * attention_normed
    attention_grad = norm_back(attention, gated_grad * update).reshape(span, heads, head).astype(BF)
    moment = product("bhc,bhe->hce", query, (attention_grad * first).astype(BF))
    after = entering(moment, carried, True)

    score_grad = (product("the,she->hts", attention_grad, value) * grid).astype(BF)
    query_grad = (
        product("hts,shc->thc", score_grad, key) + product("the,hce->thc", attention_grad, incoming) * lead
    )
    early = jnp.concatenate([turn_back(raw_query, query_grad), update_grad], axis=1).astype(BF)
    quarter = width // 4
    early_pieces = jnp.stack(
        [
            jnp.concatenate(
                [block[:, j * quarter : (j + 1) * quarter] for block in (early[:, :width], early[:, width:], mix_grad)],
                axis=1,
            )
            for j in range(4)
        ]
    )
    early_all = jnp.concatenate(exchange_tp(early_pieces, owner))
    early_part = jnp.concatenate(
        [dot_tn(normed_all, early_all[:, : 2 * quarter]), dot_tn(gated_all, early_all[:, 2 * quarter :])], axis=1
    )
    early_sum = reduce_seq(early_part)

    gate_weight = dot_tn(ffn_rows, gate_grad)
    up_weight = dot_tn(ffn_rows, up_grad)
    down_weight = dot_tn(down_grad, hidden)

    def over_seq(array):
        return lax.psum_scatter(array, "seq", scatter_dimension=0, tiled=True).astype(F32)

    gate_sum, up_sum, down_sum = over_seq(gate_weight), over_seq(up_weight), over_seq(down_weight)

    key_grad = product("hts,thc->shc", score_grad, query) + product("she,hce->shc", value, after) * rear
    value_grad = product("hts,the->she", scores, attention_grad) + product("shc,hce->she", key, after) * rear
    late = jnp.concatenate([turn_back(raw_key, key_grad), value_grad.reshape(span, width)], axis=1).astype(BF)
    late_pieces = jnp.stack(
        [
            jnp.concatenate(
                [block[:, j * quarter : (j + 1) * quarter] for block in (late[:, :width], late[:, width:])], axis=1
            )
            for j in range(4)
        ]
    )
    late_all = jnp.concatenate(exchange_tp(late_pieces, owner))
    late_sum = reduce_seq(dot_tn(normed_all, late_all))

    projected_grad = jnp.concatenate([early[:, :width], late, early[:, width:]], axis=1)
    normed_grad = dot_nt(projected_grad, w_mix)
    d_tokens = (resid_grad + norm_back(inputs, normed_grad)).astype(BF)

    early_full = collect_tp(early_sum.astype(BF), owner)
    late_full = collect_tp(late_sum.astype(BF), owner)
    mix_sum = jnp.concatenate(
        [p[:, :quarter] for p in early_full]
        + [p[:, :quarter] for p in late_full]
        + [p[:, quarter:] for p in late_full]
        + [p[:, quarter : 2 * quarter] for p in early_full],
        axis=1,
    ).astype(F32)
    out_sum = jnp.concatenate([p[:, 2 * quarter :] for p in early_full], axis=1).astype(F32)
    shape = (items, span, width)
    return (out.reshape(shape), d_tokens.reshape(shape), mix_sum, out_sum, gate_sum, up_sum, down_sum)


def solution(mesh):
    in_specs = (
        P("tp", "seq", None),
        P(),
        P(),
        P(),
        P(),
        P(None, "tp"),
        P(None, "tp"),
        P(None, "tp"),
        P("tp", "seq", None),
    )
    out_specs = (
        P("tp", "seq", None),
        P("tp", "seq", None),
        P("seq", None),
        P("seq", None),
        P("seq", "tp"),
        P("seq", "tp"),
        P("seq", "tp"),
    )
    return jax.shard_map(
        on_device, mesh=mesh, in_specs=in_specs, out_specs=out_specs, check_vma=False
    )
```

```python
from functools import partial
import math

import jax
import jax.numpy as jnp
import numpy as np
from jax import lax
from jax.experimental import pallas as pl
from jax.experimental.pallas import tpu as pltpu
from jax.sharding import PartitionSpec as P

HEADS = 8
HEAD = 128
HALF = HEADS // 2
PAIR = 2 * HEAD
EPSILON = 1e-06
BF = jnp.bfloat16
F32 = jnp.float32
SMALL = pl.BlockSpec(memory_space=pltpu.SMEM)
WHOLE = pl.BlockSpec(memory_space=pltpu.VMEM)
MIB = 1024 * 1024
ROOM = 4
SCALE = 0.01


def norm_scale(value):
    return lax.rsqrt(jnp.mean(value * value, axis=-1, keepdims=True) + EPSILON)


def norm_back(value, upstream):
    r = norm_scale(value)
    return r * upstream - value * (r * r * r * jnp.mean(value * upstream, axis=-1, keepdims=True))


def dot_nn(left, right):
    return jnp.dot(left, right, preferred_element_type=F32)


def dot_nt(left, right):
    return lax.dot_general(left, right, (((1,), (1,)), ((), ())), preferred_element_type=F32)


def dot_tn(left, right):
    return lax.dot_general(left, right, (((0,), (0,)), ((), ())), preferred_element_type=F32)


def rotation(places, width):
    table = np.floor(
        65536.0 / (2.0 * math.pi) * 10000.0 ** (-np.arange(width) / width) + 0.5
    ).astype(np.int32)
    phase = jnp.remainder(places[:, None] * jnp.asarray(table)[None, :], 65536)
    angle = phase.astype(F32) * (2.0 * math.pi / 65536.0)
    return (jnp.cos(angle), jnp.sin(angle))


def swap(array, axis, bit):
    count = lax.axis_size(axis)
    return lax.ppermute(array, axis, [(i, i ^ bit) for i in range(count)])


def tie(array, *others):
    return lax.optimization_barrier((array, *others))[0]


def positions(rows, columns):
    return lax.broadcasted_iota(jnp.int32, (rows, columns), 0).astype(F32)


def decay_grid(rate, span):
    gap = positions(span, span) - lax.broadcasted_iota(jnp.int32, (span, span), 1).astype(F32)
    return jnp.where(gap >= 0, jnp.exp(-rate * jnp.maximum(gap, 0.0)), 0.0)


def spread(values, cosine, sine):
    return jnp.concatenate([values * cosine, values * sine], axis=1).astype(BF)


def fold(grad, cosine, sine):
    return grad[:, :HEAD] * cosine + grad[:, HEAD:] * sine


def slope_of(raw):
    gate = jax.nn.sigmoid(raw)
    return gate * (1.0 + raw * (1.0 - gate))


def shape_of(shape, kind):
    return jax.ShapeDtypeStruct(shape, kind)


def params(room):
    return pltpu.CompilerParams(vmem_limit_bytes=int(room))


def cost(flops, moved):
    return pl.CostEstimate(flops=int(flops * SCALE), bytes_accessed=int(moved * SCALE), transcendentals=0)


class Line:
    def __init__(self):
        self.last = None
        self.more = []

    def wait(self, *arrays):
        self.more += arrays

    def hold(self, array):
        return array if self.last is None else tie(array, self.last)

    def swap(self, array, axis, bit):
        return swap(self.hold(array), axis, bit)

    def run(self, name, kernel, outs, scalars, arrays, flops=0):
        arrays = list(arrays)
        arrays[0] = self.hold(arrays[0])
        if self.more:
            arrays[0] = tie(arrays[0], *self.more)
            self.more = []
        moved = sum(a.size * a.dtype.itemsize for a in arrays)
        moved += sum(math.prod(s) * jnp.dtype(k).itemsize for s, k in outs)
        results = pl.pallas_call(
            kernel,
            name=name,
            out_shape=[shape_of(s, k) for s, k in outs],
            in_specs=[SMALL] * len(scalars) + [WHOLE] * len(arrays),
            out_specs=[WHOLE] * len(outs),
            compiler_params=params(moved * 1.125 + ROOM * MIB),
            cost_estimate=cost(flops, moved),
        )(*scalars, *arrays)
        self.last = results[0]
        return results


def left_of(numbers, lengths, span):
    return lengths[numbers[2]] - (2 * numbers[1] + numbers[0]) * span


def valid_rows(numbers, lengths, shape):
    return lax.broadcasted_iota(jnp.int32, shape, 0) < left_of(numbers, lengths, shape[0])


def columns_of(w_mix, block, j):
    groups = w_mix.shape[1] // (4 * PAIR)
    return w_mix[:, (block * groups + j) * PAIR : (block * groups + j + 1) * PAIR]


def key_value_kernel(numbers, forget, tokens, cosine, sine, w_mix, normed, raw_key, key, value, send, keep):
    span, width = tokens.shape
    groups = width // PAIR
    inputs = tokens[...].astype(F32)
    rows = (inputs * norm_scale(inputs)).astype(BF)
    normed[...] = rows
    place = positions(span, HEAD)
    states = []
    for g in range(groups):
        lanes = slice(g * PAIR, (g + 1) * PAIR)
        raw = dot_nn(rows, columns_of(w_mix, 1, g))
        raw_key[:, lanes] = raw
        low = dot_nn(rows, columns_of(w_mix, 2, g)).astype(BF)
        value[:, lanes] = low
        active = raw * jax.nn.sigmoid(raw)
        for h in range(2):
            part = slice(h * HEAD, (h + 1) * HEAD)
            turned = spread(active[:, part], cosine[...], sine[...])
            start = 2 * (2 * g + h) * HEAD
            key[:, start : start + 2 * HEAD] = turned
            tail = jnp.exp(-forget[2 * g + h] * (span - 1.0 - place))
            states.append(dot_tn(turned, (low[:, part].astype(F32) * tail).astype(BF)).astype(BF))
    low_side = numbers[0] == 0
    for h in range(HALF):
        keep[h] = jnp.where(low_side, states[h], states[h + HALF])
        send[h] = jnp.where(low_side, states[h + HALF], states[h])


def query_kernel(
    numbers, lengths, forget, normed, key, value, cosine, sine, w_mix, cotangent,
    raw_query, query, update, scores, intra, down_low,
):
    span, width = normed.shape
    upstream = cotangent[...]
    down_low[...] = jnp.where(valid_rows(numbers, lengths, upstream.shape), upstream, jnp.zeros_like(upstream))
    groups = width // PAIR
    rows = normed[...]
    for g in range(groups):
        lanes = slice(g * PAIR, (g + 1) * PAIR)
        raw = dot_nn(rows, columns_of(w_mix, 0, g))
        raw_query[:, lanes] = raw
        update[:, lanes] = dot_nn(rows, columns_of(w_mix, 3, g))
        active = raw * jax.nn.sigmoid(raw)
        for h in range(2):
            head = 2 * g + h
            part = slice(head * HEAD, (head + 1) * HEAD)
            wide = slice(2 * head * HEAD, 2 * (head + 1) * HEAD)
            turned = spread(active[:, h * HEAD : (h + 1) * HEAD], cosine[...], sine[...])
            query[:, wide] = turned
            low = (dot_nt(turned, key[:, wide]) * decay_grid(forget[head], span)).astype(BF)
            scores[head] = low
            intra[:, part] = dot_nn(low, value[:, part])


def stand(numbers, backward):
    side, layer = numbers[0], numbers[1]
    low = side == 1 if backward else side == 0
    depth = 3 - layer if backward else layer
    return side, low, lax.rem(depth, 2) == 0, depth < 2


def block_rate(forget, side, h, span):
    return jnp.exp(jnp.zeros((1, HEAD), F32) - forget[side * HALF + h] * span)


def pair_kernel(backward, span, numbers, forget, keep, other, pair):
    side, low, _, _ = stand(numbers, backward)
    for h in range(HALF):
        rate = block_rate(forget, side, h, span)
        mine, theirs = keep[h].astype(F32), other[h].astype(F32)
        pair[h] = (jnp.where(low, rate, 1.0) * mine + jnp.where(low, 1.0, rate) * theirs).astype(BF)


def quad_kernel(backward, span, numbers, forget, pair, near, quad):
    side, _, even, _ = stand(numbers, backward)
    for h in range(HALF):
        rate = block_rate(forget, side, h, 2.0 * span)
        mine, theirs = pair[h].astype(F32), near[h].astype(F32)
        quad[h] = (jnp.where(even, rate, 1.0) * mine + jnp.where(even, 1.0, rate) * theirs).astype(BF)


def enter_kernel(backward, span, numbers, forget, near, far, keep, other, theirs, mine):
    side, low, even, early = stand(numbers, backward)
    for h in range(HALF):
        rate = block_rate(forget, side, h, span)
        double = block_rate(forget, side, h, 2.0 * span)
        from_near = jnp.where(even, 0.0, 1.0)
        from_far = jnp.where(early, 0.0, jnp.where(even, 1.0, double))
        before = from_near * near[h].astype(F32) + from_far * far[h].astype(F32)
        added = before * rate + jnp.where(low, keep[h].astype(F32), other[h].astype(F32))
        theirs[h] = jnp.where(low, added, before).astype(BF)
        mine[h] = jnp.where(low, before, added).astype(BF)


def scan_states(line, send, keep, numbers, forget, span, backward, fillers):
    name = "back" if backward else "fore"
    state = [(keep.shape, BF)]
    other = swap(send, "seq", 1)
    fillers[0](None)
    pair = line.run(name + "_pair", partial(pair_kernel, backward, span), state, [numbers, forget], [keep, other])[0]
    near = swap(pair, "seq", 2)
    fillers[1](other)
    quad = line.run(name + "_quad", partial(quad_kernel, backward, span), state, [numbers, forget], [pair, near])[0]
    far = swap(quad, "seq", 4)
    fillers[2](near)
    theirs, mine = line.run(
        name + "_enter", partial(enter_kernel, backward, span), state * 2, [numbers, forget], [near, far, keep, other]
    )
    theirs = swap(theirs, "seq", 1)
    fillers[3](far)
    return mine, theirs


def scan_any(state, forget, span, backward):
    count = lax.axis_size("seq")
    place = lax.axis_index("seq")
    ahead = count - 1 - place if backward else place
    carried = jnp.exp(-forget * span)[:, None, None]
    gathered = lax.all_gather(state, "seq")

    def one(hop, total):
        source = count - 1 - hop if backward else hop
        return total * carried + lax.dynamic_index_in_dim(gathered, source, 0, False).astype(F32)

    return lax.fori_loop(0, ahead, one, jnp.zeros(state.shape, F32)).astype(BF)


def by_side(side, mine, theirs):
    low = side == 0
    return jnp.where(low, jnp.concatenate([mine, theirs]), jnp.concatenate([theirs, mine]))


def scan(line, send, keep, numbers, forget, span, backward, fillers):
    if lax.axis_size("seq") == 8:
        return scan_states(line, send, keep, numbers, forget, span, backward, fillers)
    for filler in fillers:
        filler(None)
    whole = scan_any(by_side(numbers[0], keep, send), forget, span, backward)
    upper = numbers[0] == 0
    return jnp.where(upper, whole[:HALF], whole[HALF:]), jnp.where(upper, whole[HALF:], whole[:HALF])


def state_of(numbers, mine, theirs, h):
    first, second = (mine, theirs) if h < HALF else (theirs, mine)
    return jnp.where(numbers[0] == 0, first[h % HALF], second[h % HALF])


def mix_kernel(numbers, forget, theirs, mine, query, intra, update, tokens, w_out, attention, gated, resid, ffn_in):
    span, width = tokens.shape
    place = positions(span, HEAD)
    for h in range(HEADS):
        lanes = slice(h * HEAD, (h + 1) * HEAD)
        wide = slice(2 * h * HEAD, 2 * (h + 1) * HEAD)
        lead = jnp.exp(-forget[h] * (place + 1.0))
        attention[:, lanes] = intra[:, lanes] + dot_nn(query[:, wide], state_of(numbers, mine, theirs, h)) * lead
    whole = attention[...]
    low = (whole * norm_scale(whole) * update[...]).astype(BF)
    gated[...] = low
    after = tokens[...].astype(F32) + dot_nn(low, w_out[...])
    resid[...] = after
    ffn_in[...] = (after * norm_scale(after)).astype(BF)


def ffn_kernel(rows_0, rows_1, hidden_grad, w_gate, w_up, hidden, gate_grad, up_grad, back_0, back_1):
    span = rows_0.shape[0]
    for i, (rows, back) in enumerate(((rows_0, back_0), (rows_1, back_1))):
        block = slice(i * span, (i + 1) * span)
        gate_pre = dot_nt(rows[...], w_gate[...])
        up_pre = dot_nt(rows[...], w_up[...])
        hidden[block] = (gate_pre * up_pre).astype(BF)
        upstream = hidden_grad[block]
        gate_low = (upstream * up_pre).astype(BF)
        up_low = (upstream * gate_pre).astype(BF)
        gate_grad[block] = gate_low
        up_grad[block] = up_low
        back[...] = (dot_nn(gate_low, w_gate[...]) + dot_nn(up_low, w_up[...])).astype(BF)


def hidden_grad_kernel(rows_0, rows_1, rows_2, rows_3, w_down, near, far):
    span = rows_0.shape[0]
    for rows, target, block in (
        (rows_0, near, slice(0, span)),
        (rows_1, near, slice(span, 2 * span)),
        (rows_2, far, slice(0, span)),
        (rows_3, far, slice(span, 2 * span)),
    ):
        target[block] = dot_nt(rows[...], w_down[...])


def down_kernel(hidden_near, hidden_far, w_down, own, other, far, cross):
    span = own.shape[0]
    for source, target, block in (
        (hidden_near, own, slice(0, span)),
        (hidden_near, other, slice(span, 2 * span)),
        (hidden_far, far, slice(0, span)),
        (hidden_far, cross, slice(span, 2 * span)),
    ):
        target[...] = dot_nn(source[block], w_down[...]).astype(BF)


def add_kernel(first, second, total):
    total[...] = (first[...].astype(F32) + second[...].astype(F32)).astype(BF)


def out_kernel(numbers, lengths, part_0, part_1, part_2, resid, out):
    valid = valid_rows(numbers, lengths, resid.shape)
    down = part_0[...].astype(F32) + part_1[...].astype(F32) + part_2[...].astype(F32)
    out[...] = jnp.where(valid, resid[...] + down, 0.0).astype(BF)


def resid_kernel(
    forget, numbers, part_0, part_1, part_2, resid, down_low, attention, update, query, w_out,
    resid_grad, mix_grad, update_grad, attention_grad, send, keep,
):
    span, width = resid.shape
    ffn_grad = part_0[...].astype(F32) + part_1[...].astype(F32) + part_2[...].astype(F32)
    total = down_low[...].astype(F32) + norm_back(resid[...], ffn_grad)
    resid_grad[...] = total
    low = total.astype(BF)
    mix_grad[...] = low
    gated_grad = dot_nt(low, w_out[...])
    whole = attention[...]
    r = norm_scale(whole)
    update_grad[...] = (gated_grad * (whole * r)).astype(BF)
    upstream = gated_grad * update[...]
    back = r * upstream - whole * (r * r * r * jnp.mean(whole * upstream, axis=-1, keepdims=True))
    attention_grad[...] = back.astype(BF)
    place = positions(span, HEAD)
    moments = []
    for h in range(HEADS):
        lanes = slice(h * HEAD, (h + 1) * HEAD)
        wide = slice(2 * h * HEAD, 2 * (h + 1) * HEAD)
        first = jnp.exp(-forget[h] * place)
        moments.append(dot_tn(query[:, wide], (attention_grad[:, lanes].astype(F32) * first).astype(BF)).astype(BF))
    low_side = numbers[0] == 0
    for h in range(HALF):
        keep[h] = jnp.where(low_side, moments[h], moments[h + HALF])
        send[h] = jnp.where(low_side, moments[h + HALF], moments[h])


def early_kernel(
    numbers, forget, grad, value, key, query, scores, theirs, mine, raw_query, cosine, sine, update_grad, mix_grad,
    piece_0, piece_1, piece_2, piece_3, key_part, value_part, pieces,
):
    span, width = update_grad.shape
    place = positions(span, 2 * HEAD)
    for h in range(HEADS):
        lanes = slice(h * HEAD, (h + 1) * HEAD)
        wide = slice(2 * h * HEAD, 2 * (h + 1) * HEAD)
        upstream = grad[:, lanes]
        low = (dot_nt(upstream, value[:, lanes]) * decay_grid(forget[h], span)).astype(BF)
        lead = jnp.exp(-forget[h] * (place + 1.0))
        query_grad = dot_nn(low, key[:, wide]) + dot_nt(upstream, state_of(numbers, mine, theirs, h)) * lead
        slope = slope_of(raw_query[:, lanes])
        start = (h % 2) * HEAD
        pieces[h // 2, :, start : start + HEAD] = (slope * fold(query_grad, cosine[...], sine[...])).astype(BF)
        key_part[:, lanes] = fold(dot_tn(low, query[:, wide]), cosine[...], sine[...])
        value_part[:, lanes] = dot_tn(scores[h], upstream)
    for j in range(width // PAIR):
        columns = slice(j * PAIR, (j + 1) * PAIR)
        pieces[j, :, PAIR : 2 * PAIR] = update_grad[:, columns]
        pieces[j, :, 2 * PAIR :] = mix_grad[:, columns]
    for k, piece in enumerate((piece_0, piece_1, piece_2, piece_3)):
        piece[...] = pieces[numbers[2] ^ k]


def late_kernel(
    numbers, forget, theirs, mine, value, key, raw_key, cosine, sine, key_part, value_part,
    piece_0, piece_1, piece_2, piece_3, pieces,
):
    span, width = value.shape
    place = positions(span, HEAD)
    for h in range(HEADS):
        lanes = slice(h * HEAD, (h + 1) * HEAD)
        wide = slice(2 * h * HEAD, 2 * (h + 1) * HEAD)
        after = state_of(numbers, mine, theirs, h)
        rear = jnp.exp(-forget[h] * (span - place))
        key_grad = fold(dot_nt(value[:, lanes], after), cosine[...], sine[...]) * rear + key_part[:, lanes]
        value_grad = dot_nn(key[:, wide], after) * rear + value_part[:, lanes]
        start = (h % 2) * HEAD
        pieces[h // 2, :, start : start + HEAD] = (slope_of(raw_key[:, lanes]) * key_grad).astype(BF)
        pieces[h // 2, :, PAIR + start : PAIR + start + HEAD] = value_grad.astype(BF)
    for k, piece in enumerate((piece_0, piece_1, piece_2, piece_3)):
        piece[...] = pieces[numbers[2] ^ k]


BITS = {"y": 1, "z1": 2, "z2": 4}


def bit_of(numbers, name):
    return numbers[0] if name == "y" else numbers[1] % 2 if name == "z1" else numbers[1] // 2


def split_blocks(order, numbers, keep, send, parts, index):
    mine = bit_of(numbers, order[0]) == 0
    for place in range(4):
        rest = BITS[order[1]] * (place // 2) + BITS[order[2]] * (place % 2)
        zero, one = parts[rest], parts[rest + BITS[order[0]]]
        keep[(place, *index)] = jnp.where(mine, zero, one)
        send[(place, *index)] = jnp.where(mine, one, zero)


def mix_weight_kernel(groups, order, numbers, *refs):
    inputs, send, keep = refs[:-2], refs[-2], refs[-1]
    part = keep.shape[1]
    start = 0
    for left, right, low, high in groups:
        total = None
        for a, b in zip(left, right):
            term = dot_tn(inputs[a][...], inputs[b][:, low:high])
            total = term if total is None else total + term
        parts = [total[m * part : (m + 1) * part].astype(BF) for m in range(8)]
        split_blocks(order, numbers, keep, send, parts, (slice(None), slice(start, start + high - low)))
        start += high - low


def ffn_weight_kernel(order, numbers, *refs):
    near, far, rows, send, keep = refs[0], refs[1], refs[2:6], refs[-2], refs[-1]
    span = rows[0].shape[0]
    units = near.shape[1]
    part = keep.shape[2]
    step = 256
    for low in range(0, units, step):
        high = min(low + step, units)
        total = None
        for i in range(4):
            source = near if i < 2 else far
            term = dot_tn(source[(i % 2) * span : (i % 2 + 1) * span, low:high], rows[i][...])
            total = term if total is None else total + term
        parts = [total[:, m * part : (m + 1) * part].astype(BF) for m in range(8)]
        split_blocks(order, numbers, keep, send, parts, (slice(low, high), slice(None)))


def whole_mix_weight_kernel(groups, numbers, *refs):
    inputs, target = refs[:-1], refs[-1]
    start = 0
    for left, right, low, high in groups:
        total = None
        for a, b in zip(left, right):
            term = dot_tn(inputs[a][...], inputs[b][:, low:high])
            total = term if total is None else total + term
        target[:, start : start + high - low] = total.astype(BF)
        start += high - low


def whole_ffn_weight_kernel(numbers, *refs):
    near, far, rows, target = refs[0], refs[1], refs[2:6], refs[-1]
    span = rows[0].shape[0]
    total = None
    for i in range(4):
        source = near if i < 2 else far
        term = dot_tn(source[(i % 2) * span : (i % 2 + 1) * span], rows[i][...])
        total = term if total is None else total + term
    target[...] = total.astype(BF)


def join_kernel(name, numbers, other, keep, send, own):
    mine = bit_of(numbers, name)
    count = own.shape[0]
    for i in range(count):
        for target, half in ((own, mine), (send, 1 - mine)):
            total = keep[half * count + i].astype(F32) + other[half * count + i].astype(F32)
            target[i] = total.astype(target.dtype)


def sum_kernel(other, keep, total):
    total[...] = (keep[0].astype(F32) + other[0].astype(F32)).astype(total.dtype)


class Reduction:
    def __init__(self, line, name, numbers, order, blocks_first, kernel, whole_kernel, shape, arrays, flops):
        self.line, self.name, self.numbers, self.order = line, name, numbers, order
        self.fast = lax.axis_size("seq") == 8
        self.blocks_first = blocks_first
        if self.fast:
            rows, columns = shape
            block = (rows // 8, columns) if blocks_first else (rows, columns // 8)
            outs = [((4, *block), BF)] * 2
            self.send, self.keep = line.run(name, partial(kernel, order), outs, [numbers], arrays, flops)
        else:
            self.whole = line.run(name, whole_kernel, [(shape, BF)], [numbers], arrays, flops)[0]
        self.step = 0
        if not self.fast:
            self.send = self.whole

    def go(self):
        if self.fast:
            self.other = self.line.swap(self.send, "seq", BITS[self.order[self.step]])

    def wait(self):
        if self.fast:
            self.line.wait(self.other)

    def join(self):
        self.step += 1
        if self.fast:
            count, *block = self.keep.shape
            kind = F32 if count == 2 else BF
            self.send, self.keep = self.line.run(
                f"{self.name}_join{self.step}",
                partial(join_kernel, self.order[self.step]),
                [((count // 2, *block), BF), ((count // 2, *block), kind)],
                [self.numbers],
                [self.other, self.keep],
            )

    def total(self, kind):
        if self.fast:
            block = self.keep.shape[1:]
            return self.line.run(self.name + "_sum", sum_kernel, [(block, kind)], [], [self.other, self.keep])[0]
        return lax.psum_scatter(
            self.whole, "seq", scatter_dimension=0 if self.blocks_first else 1, tiled=True
        ).astype(kind)


def normed_grad_kernel(pieces, w_mix, target):
    total = None
    count = pieces.shape[0]
    for j in range(count):
        for source, block in ((0, 0), (1, 3)):
            term = dot_nt(pieces[j, :, source * PAIR : (source + 1) * PAIR], columns_of(w_mix, block, j))
            total = term if total is None else total + term
    target[...] = total


def tokens_kernel(pieces, early, resid_grad, tokens, w_mix, target):
    total = early[...]
    count = pieces.shape[0]
    for j in range(count):
        for source, block in ((0, 1), (1, 2)):
            total = total + dot_nt(pieces[j, :, source * PAIR : (source + 1) * PAIR], columns_of(w_mix, block, j))
    target[...] = (resid_grad[...] + norm_back(tokens[...].astype(F32), total)).astype(BF)


def gather_far(array):
    far = swap(array, "tp", 2)
    return [array, swap(array, "tp", 1), far, swap(far, "tp", 1)]


def collect_kernel(numbers, *refs):
    early, late, mix, out = refs[1:5], (*refs[5:8], refs[0]), refs[8], refs[9]
    quarter = out.shape[1] // 4
    width = out.shape[1]
    owner = numbers[2]

    def pick(parts, j, block):
        columns = slice(block * quarter, (block + 1) * quarter)
        a, b, c, d = (parts[j ^ k][:, columns].astype(F32) for k in range(4))
        return jnp.where(owner < 2, jnp.where(owner == 0, a, b), jnp.where(owner == 2, c, d))

    for j in range(4):
        columns = lambda block: slice(block * width + j * quarter, block * width + (j + 1) * quarter)
        mix[:, columns(0)] = pick(early, j, 0)
        mix[:, columns(1)] = pick(late, j, 0)
        mix[:, columns(2)] = pick(late, j, 1)
        mix[:, columns(3)] = pick(early, j, 1)
        out[:, columns(0)] = pick(early, j, 2)


def on_device(tokens, lengths, forget, w_mix, w_out, w_gate, w_up, w_down, cotangent):
    shape = tokens.shape
    _, span, width = shape
    units = w_gate.shape[1]
    quarter = width // 4
    place = lax.axis_index("seq")
    owner = lax.axis_index("tp")
    numbers = jnp.stack([place % 2, place // 2, owner]).astype(jnp.int32)
    cosine, sine = rotation(place * span + jnp.arange(span, dtype=jnp.int32), HEAD)
    tokens = tokens.reshape(span, width)
    cotangent = cotangent.reshape(span, width)
    w_gate, w_up, w_down = w_gate.T, w_up.T, w_down.T
    small = (span, width)
    state = ((HALF, 2 * HEAD, HEAD), BF)
    line = Line()
    got = {}

    normed, raw_key, key, value, send, keep = line.run(
        "key_value",
        key_value_kernel,
        [(small, BF), (small, F32), ((span, 2 * width), BF), (small, BF), state, state],
        [numbers, forget],
        [tokens, cosine, sine, w_mix],
        4 * span * width * width,
    )
    line.last = normed

    def fore_1(_):
        got["query"] = line.run(
            "query",
            query_kernel,
            [(small, F32), ((span, 2 * width), BF), (small, F32), ((HEADS, span, span), BF), (small, F32), (small, BF)],
            [numbers, lengths, forget],
            [normed, key, value, cosine, sine, w_mix, cotangent],
            6 * span * width * width,
        )

    def fore_2(other):
        got["down_far"] = line.swap(got["query"][5], "tp", 2)

    def fore_3(near):
        got["normed_far"] = line.swap(normed, "tp", 2)
        got["down_near"] = line.swap(got["query"][5], "tp", 1)
        line.wait(got["down_far"], got["down_near"])

    def fore_4(far):
        got["down_cross"] = line.swap(got["down_far"], "tp", 1)
        line.wait(got["down_cross"], got["normed_far"])

    mine, theirs = scan(line, send, keep, numbers, forget, span, False, (fore_1, fore_2, fore_3, fore_4))
    raw_query, query, update, scores, intra, down_low = got["query"]
    down_rows = [down_low, got["down_near"], got["down_far"], got["down_cross"]]

    attention, gated, resid, ffn_in = line.run(
        "mix",
        mix_kernel,
        [(small, F32), (small, BF), (small, F32), (small, BF)],
        [numbers, forget],
        [theirs, mine, query, intra, update, tokens, w_out],
        2 * span * width * width * 1.25,
    )
    ffn_rows = [ffn_in, line.swap(ffn_in, "tp", 1), line.swap(ffn_in, "tp", 2)]
    normed_rows = [normed, line.swap(normed, "tp", 1), got["normed_far"], line.swap(got["normed_far"], "tp", 1)]
    gated_near = line.swap(gated, "tp", 1)
    hidden_grad = line.run(
        "hidden_grad", hidden_grad_kernel, [((2 * span, units), F32)] * 2, [], [*down_rows, w_down],
        8 * span * width * units,
    )

    def ffn(name, first, second, upstream):
        return line.run(
            name,
            lambda rows_1, rows_0, *rest: ffn_kernel(rows_0, rows_1, *rest),
            [((2 * span, units), BF)] * 3 + [(small, BF)] * 2,
            [],
            [second, first, upstream, w_gate, w_up],
            16 * span * width * units,
        )

    line.wait(normed_rows[1], normed_rows[3], gated_near)
    hidden_near, gate_near, up_near, back_0, back_1 = ffn("ffn_near", ffn_rows[0], ffn_rows[1], hidden_grad[0])
    ffn_rows.append(line.swap(ffn_rows[2], "tp", 1))
    hidden_far, gate_far, up_far, back_2, back_3 = ffn("ffn_far", ffn_rows[2], ffn_rows[3], hidden_grad[1])
    part_1, from_3 = line.swap(back_1, "tp", 1), line.swap(back_3, "tp", 1)

    def ffn_weight(name, order, near, far, rows):
        return Reduction(
            line, name, numbers, order, False, ffn_weight_kernel, whole_ffn_weight_kernel, (units, width),
            [near, far, *rows], 8 * span * width * units,
        )

    y_first, z_first = ("y", "z1", "z2"), ("z1", "y", "z2")
    gate_sum = ffn_weight("d_gate", y_first, gate_near, gate_far, ffn_rows)
    gate_sum.go()
    line.wait(part_1)
    part_2 = line.run("ffn_add", add_kernel, [(small, BF)], [], [from_3, back_2])[0]
    part_2 = line.swap(part_2, "tp", 2)
    down_sum = ffn_weight("d_down", z_first, hidden_near, hidden_far, down_rows)
    down_sum.go()
    downs = line.run(
        "down", down_kernel, [(small, BF)] * 4, [], [hidden_near, hidden_far, w_down], 8 * span * width * units
    )
    down_1, down_3 = line.swap(downs[1], "tp", 1), line.swap(downs[3], "tp", 1)
    up_sum = ffn_weight("d_up", y_first, up_near, up_far, ffn_rows)
    resid_grad, mix_grad, update_grad, attention_grad, send, keep = line.run(
        "resid",
        resid_kernel,
        [(small, F32), (small, BF), (small, BF), (small, BF), state, state],
        [forget, numbers],
        [part_2, back_0, part_1, resid, down_low, attention, update, query, w_out],
        2 * span * width * width * 1.25,
    )

    def mix_weight(name, groups, arrays, columns):
        return Reduction(
            line, name, numbers, y_first, True,
            lambda order, *refs: mix_weight_kernel(groups, order, *refs),
            partial(whole_mix_weight_kernel, groups),
            (width, columns), arrays, 8 * span * width * columns,
        )

    four, more, most = (0, 1, 2, 3), (4, 5, 6, 7), (8, 9, 10, 11)

    def back_1_(_):
        got["gated_far"] = line.swap(gated, "tp", 2)
        gate_sum.wait()
        line.wait(down_1, down_3)
        got["early"] = line.run(
            "early",
            early_kernel,
            [((span, 3 * quarter), BF)] * 4 + [(small, F32)] * 2 + [((4, span, 3 * quarter), BF)],
            [numbers, forget],
            [attention_grad, value, key, query, scores, theirs, mine, raw_query, cosine, sine, update_grad, mix_grad],
            12 * span * span * width,
        )
        got["early_2"], got["early_3"] = line.swap(got["early"][2], "tp", 2), line.swap(got["early"][3], "tp", 3)
        got["down_2"] = line.run("down_add", add_kernel, [(small, BF)], [], [down_3, downs[2]])[0]
        down_sum.wait()

    def back_2_(other):
        up_sum.go()
        line.wait(got["gated_far"])

    def back_3_(near):
        gate_sum.join()
        gate_sum.go()
        line.wait(got["early_2"], got["early_3"])
        got["normed_grad"] = line.run(
            "normed_grad", normed_grad_kernel, [(small, F32)], [], [got["early"][6], w_mix], 4 * span * width * width
        )[0]
        got["early_1"], got["gated_cross"] = line.swap(got["early"][1], "tp", 1), line.swap(got["gated_far"], "tp", 1)
        up_sum.wait()

    def back_4_(far):
        up_sum.join()
        up_sum.go()
        down_sum.join()
        down_sum.go()
        got["early_sum"] = mix_weight(
            "d_early",
            [(most, four, 0, 2 * quarter), (more, four, 2 * quarter, 3 * quarter)],
            [got["early_1"], got["early"][0], got["early_2"], got["early_3"]]
            + [gated_near, gated, got["gated_far"], got["gated_cross"]]
            + [normed_rows[k] for k in (1, 0, 2, 3)],
            3 * quarter,
        )
        gate_sum.join()
        gate_sum.go()

    after_mine, after_theirs = scan(
        line, send, keep, numbers, forget, span, True, (back_1_, back_2_, back_3_, back_4_)
    )
    key_part, value_part = got["early"][4:6]
    early_sum = got["early_sum"]
    *late, late_pieces = line.run(
        "late",
        late_kernel,
        [((span, 2 * quarter), BF)] * 4 + [((4, span, 2 * quarter), BF)],
        [numbers, forget],
        [after_theirs, after_mine, value, key, raw_key, cosine, sine, key_part, value_part],
        4 * span * span * width,
    )
    late_2, late_3 = line.swap(late[2], "tp", 2), line.swap(late[3], "tp", 3)
    up_sum.join()
    up_sum.go()
    down_sum.join()
    down_sum.go()
    gate_grad = gate_sum.total(F32)
    early_sum.go()
    late_1 = line.swap(late[1], "tp", 1)
    line.wait(late_2, late_3)
    late_sum = mix_weight(
        "d_late",
        [(more, four, 0, 2 * quarter)],
        [late_1, late[0], late_2, late_3] + [normed_rows[k] for k in (1, 0, 2, 3)],
        2 * quarter,
    )
    late_sum.go()
    down_2 = line.swap(got["down_2"], "tp", 2)
    up_grad = up_sum.total(F32)
    d_tokens = line.run(
        "d_tokens",
        tokens_kernel,
        [(small, BF)],
        [],
        [late_pieces, got["normed_grad"], resid_grad, tokens, w_mix],
        4 * span * width * width,
    )[0]
    down_grad = down_sum.total(F32)
    early_sum.join()
    early_sum.go()
    out = line.run("out", out_kernel, [(small, BF)], [numbers, lengths], [down_2, downs[0], down_1, resid])[0]
    early_sum.join()
    early_sum.go()
    late_sum.join()
    late_sum.go()
    late_sum.join()
    late_sum.go()
    early_full = gather_far(early_sum.total(BF))
    late_full = gather_far(late_sum.total(BF))
    rows = early_full[0].shape[0]
    mix_sum, out_sum = line.run(
        "collect",
        collect_kernel,
        [((rows, 4 * width), F32), ((rows, width), F32)],
        [numbers],
        [late_full[3], *early_full, *late_full[:3]],
    )
    return (out.reshape(shape), d_tokens.reshape(shape), mix_sum, out_sum, gate_grad.T, up_grad.T, down_grad.T)


def solution(mesh):
    in_specs = (
        P("tp", "seq", None),
        P(),
        P(),
        P(),
        P(),
        P(None, "tp"),
        P(None, "tp"),
        P(None, "tp"),
        P("tp", "seq", None),
    )
    out_specs = (
        P("tp", "seq", None),
        P("tp", "seq", None),
        P("seq", None),
        P("seq", None),
        P("seq", "tp"),
        P("seq", "tp"),
        P("seq", "tp"),
    )
    return jax.shard_map(
        on_device, mesh=mesh, in_specs=in_specs, out_specs=out_specs, check_vma=False
    )
```

```python
from functools import partial
import math

import jax
import jax.numpy as jnp
import numpy as np
from jax import lax
from jax.experimental import pallas as pl
from jax.experimental.pallas import tpu as pltpu
from jax.sharding import PartitionSpec as P

HEADS = 8
HEAD = 128
HALF = HEADS // 2
PAIR = 2 * HEAD
EPSILON = 1e-06
BF = jnp.bfloat16
F32 = jnp.float32
SMALL = pl.BlockSpec(memory_space=pltpu.SMEM)
WHOLE = pl.BlockSpec(memory_space=pltpu.VMEM)
MIB = 1024 * 1024
ROOM = 4
BRIEF = 0.02
LONG = 6.0


def norm_scale(value):
    return lax.rsqrt(jnp.mean(value * value, axis=-1, keepdims=True) + EPSILON)


def norm_back(value, upstream):
    r = norm_scale(value)
    return r * upstream - value * (r * r * r * jnp.mean(value * upstream, axis=-1, keepdims=True))


def dot_nn(left, right):
    return jnp.dot(left, right, preferred_element_type=F32)


def dot_nt(left, right):
    return lax.dot_general(left, right, (((1,), (1,)), ((), ())), preferred_element_type=F32)


def dot_tn(left, right):
    return lax.dot_general(left, right, (((0,), (0,)), ((), ())), preferred_element_type=F32)


def rotation(places, width):
    table = np.floor(
        65536.0 / (2.0 * math.pi) * 10000.0 ** (-np.arange(width) / width) + 0.5
    ).astype(np.int32)
    phase = jnp.remainder(places[:, None] * jnp.asarray(table)[None, :], 65536)
    angle = phase.astype(F32) * (2.0 * math.pi / 65536.0)
    return (jnp.cos(angle), jnp.sin(angle))


def swap(array, axis, bit):
    count = lax.axis_size(axis)
    return lax.ppermute(array, axis, [(i, i ^ bit) for i in range(count)])


def tie(array, *others):
    return lax.optimization_barrier((array, *others))[0]


def positions(rows, columns):
    return lax.broadcasted_iota(jnp.int32, (rows, columns), 0).astype(F32)


def decay_grid(rate, span):
    gap = positions(span, span) - lax.broadcasted_iota(jnp.int32, (span, span), 1).astype(F32)
    return jnp.where(gap >= 0, jnp.exp(-rate * jnp.maximum(gap, 0.0)), 0.0)


def spread(values, cosine, sine):
    return jnp.concatenate([values * cosine, values * sine], axis=1).astype(BF)


def fold(grad, cosine, sine):
    return grad[:, :HEAD] * cosine + grad[:, HEAD:] * sine


def slope_of(raw):
    gate = jax.nn.sigmoid(raw)
    return gate * (1.0 + raw * (1.0 - gate))


def shape_of(shape, kind):
    return jax.ShapeDtypeStruct(shape, kind)


def params(room):
    return pltpu.CompilerParams(vmem_limit_bytes=int(room))


def cost(span_us):
    return pl.CostEstimate(flops=int(span_us * 1.1e9), bytes_accessed=1024, transcendentals=0)


class Line:
    def __init__(self):
        self.last = None
        self.more = []

    def wait(self, *arrays):
        self.more += arrays

    def hold(self, array):
        return array if self.last is None else tie(array, self.last)

    def swap(self, array, axis, bit):
        return swap(self.hold(array), axis, bit)

    def run(self, name, kernel, outs, scalars, arrays, time=BRIEF):
        arrays = list(arrays)
        arrays[0] = self.hold(arrays[0])
        if self.more:
            arrays[0] = tie(arrays[0], *self.more)
            self.more = []
        moved = sum(a.size * a.dtype.itemsize for a in arrays)
        moved += sum(math.prod(s) * jnp.dtype(k).itemsize for s, k in outs)
        results = pl.pallas_call(
            kernel,
            name=name,
            out_shape=[shape_of(s, k) for s, k in outs],
            in_specs=[SMALL] * len(scalars) + [WHOLE] * len(arrays),
            out_specs=[WHOLE] * len(outs),
            compiler_params=params(moved * 1.125 + ROOM * MIB),
            cost_estimate=cost(time),
        )(*scalars, *arrays)
        self.last = results[0]
        return results


def left_of(numbers, lengths, span):
    return lengths[numbers[2]] - (2 * numbers[1] + numbers[0]) * span


def valid_rows(numbers, lengths, shape):
    return lax.broadcasted_iota(jnp.int32, shape, 0) < left_of(numbers, lengths, shape[0])


def columns_of(w_mix, block, j):
    groups = w_mix.shape[1] // (4 * PAIR)
    return w_mix[:, (block * groups + j) * PAIR : (block * groups + j + 1) * PAIR]


def key_value_kernel(numbers, forget, tokens, cosine, sine, w_mix, normed, raw_key, key, value, send, keep):
    span, width = tokens.shape
    groups = width // PAIR
    inputs = tokens[...].astype(F32)
    rows = (inputs * norm_scale(inputs)).astype(BF)
    normed[...] = rows
    place = positions(span, HEAD)
    states = []
    for g in range(groups):
        lanes = slice(g * PAIR, (g + 1) * PAIR)
        raw = dot_nn(rows, columns_of(w_mix, 1, g))
        raw_key[:, lanes] = raw
        low = dot_nn(rows, columns_of(w_mix, 2, g)).astype(BF)
        value[:, lanes] = low
        active = raw * jax.nn.sigmoid(raw)
        for h in range(2):
            part = slice(h * HEAD, (h + 1) * HEAD)
            turned = spread(active[:, part], cosine[...], sine[...])
            start = 2 * (2 * g + h) * HEAD
            key[:, start : start + 2 * HEAD] = turned
            tail = jnp.exp(-forget[2 * g + h] * (span - 1.0 - place))
            states.append(dot_tn(turned, (low[:, part].astype(F32) * tail).astype(BF)).astype(BF))
    low_side = numbers[0] == 0
    for h in range(HALF):
        keep[h] = jnp.where(low_side, states[h], states[h + HALF])
        send[h] = jnp.where(low_side, states[h + HALF], states[h])


def query_kernel(
    numbers, lengths, forget, normed, key, value, cosine, sine, w_mix, cotangent,
    raw_query, query, update, scores, intra, down_low,
):
    span, width = normed.shape
    upstream = cotangent[...]
    down_low[...] = jnp.where(valid_rows(numbers, lengths, upstream.shape), upstream, jnp.zeros_like(upstream))
    groups = width // PAIR
    rows = normed[...]
    for g in range(groups):
        lanes = slice(g * PAIR, (g + 1) * PAIR)
        raw = dot_nn(rows, columns_of(w_mix, 0, g))
        raw_query[:, lanes] = raw
        update[:, lanes] = dot_nn(rows, columns_of(w_mix, 3, g))
        active = raw * jax.nn.sigmoid(raw)
        for h in range(2):
            head = 2 * g + h
            part = slice(head * HEAD, (head + 1) * HEAD)
            wide = slice(2 * head * HEAD, 2 * (head + 1) * HEAD)
            turned = spread(active[:, h * HEAD : (h + 1) * HEAD], cosine[...], sine[...])
            query[:, wide] = turned
            low = (dot_nt(turned, key[:, wide]) * decay_grid(forget[head], span)).astype(BF)
            scores[head] = low
            intra[:, part] = dot_nn(low, value[:, part])


def stand(numbers, backward):
    side, layer = numbers[0], numbers[1]
    low = side == 1 if backward else side == 0
    depth = 3 - layer if backward else layer
    return side, low, lax.rem(depth, 2) == 0, depth < 2


def block_rate(forget, side, h, span):
    return jnp.exp(jnp.zeros((1, HEAD), F32) - forget[side * HALF + h] * span)


def pair_kernel(backward, span, numbers, forget, keep, other, pair):
    side, low, _, _ = stand(numbers, backward)
    for h in range(HALF):
        rate = block_rate(forget, side, h, span)
        mine, theirs = keep[h].astype(F32), other[h].astype(F32)
        pair[h] = (jnp.where(low, rate, 1.0) * mine + jnp.where(low, 1.0, rate) * theirs).astype(BF)


def quad_kernel(backward, span, numbers, forget, pair, near, quad):
    side, _, even, _ = stand(numbers, backward)
    for h in range(HALF):
        rate = block_rate(forget, side, h, 2.0 * span)
        mine, theirs = pair[h].astype(F32), near[h].astype(F32)
        quad[h] = (jnp.where(even, rate, 1.0) * mine + jnp.where(even, 1.0, rate) * theirs).astype(BF)


def enter_kernel(backward, span, numbers, forget, near, far, keep, other, theirs, mine):
    side, low, even, early = stand(numbers, backward)
    for h in range(HALF):
        rate = block_rate(forget, side, h, span)
        double = block_rate(forget, side, h, 2.0 * span)
        from_near = jnp.where(even, 0.0, 1.0)
        from_far = jnp.where(early, 0.0, jnp.where(even, 1.0, double))
        before = from_near * near[h].astype(F32) + from_far * far[h].astype(F32)
        added = before * rate + jnp.where(low, keep[h].astype(F32), other[h].astype(F32))
        theirs[h] = jnp.where(low, added, before).astype(BF)
        mine[h] = jnp.where(low, before, added).astype(BF)


def scan_states(line, send, keep, numbers, forget, span, backward, fillers):
    name = "back" if backward else "fore"
    state = [(keep.shape, BF)]
    other = swap(send, "seq", 1)
    fillers[0](None)
    pair = line.run(name + "_pair", partial(pair_kernel, backward, span), state, [numbers, forget], [keep, other])[0]
    near = swap(pair, "seq", 2)
    fillers[1](other)
    quad = line.run(name + "_quad", partial(quad_kernel, backward, span), state, [numbers, forget], [pair, near])[0]
    far = swap(quad, "seq", 4)
    fillers[2](near)
    theirs, mine = line.run(
        name + "_enter", partial(enter_kernel, backward, span), state * 2, [numbers, forget], [near, far, keep, other]
    )
    theirs = swap(theirs, "seq", 1)
    fillers[3](far)
    return mine, theirs


def scan_any(state, forget, span, backward):
    count = lax.axis_size("seq")
    place = lax.axis_index("seq")
    ahead = count - 1 - place if backward else place
    carried = jnp.exp(-forget * span)[:, None, None]
    gathered = lax.all_gather(state, "seq")

    def one(hop, total):
        source = count - 1 - hop if backward else hop
        return total * carried + lax.dynamic_index_in_dim(gathered, source, 0, False).astype(F32)

    return lax.fori_loop(0, ahead, one, jnp.zeros(state.shape, F32)).astype(BF)


def by_side(side, mine, theirs):
    low = side == 0
    return jnp.where(low, jnp.concatenate([mine, theirs]), jnp.concatenate([theirs, mine]))


def scan(line, send, keep, numbers, forget, span, backward, fillers):
    if lax.axis_size("seq") == 8:
        return scan_states(line, send, keep, numbers, forget, span, backward, fillers)
    for filler in fillers:
        filler(None)
    whole = scan_any(by_side(numbers[0], keep, send), forget, span, backward)
    upper = numbers[0] == 0
    return jnp.where(upper, whole[:HALF], whole[HALF:]), jnp.where(upper, whole[HALF:], whole[:HALF])


def state_of(numbers, mine, theirs, h):
    first, second = (mine, theirs) if h < HALF else (theirs, mine)
    return jnp.where(numbers[0] == 0, first[h % HALF], second[h % HALF])


def mix_kernel(numbers, forget, theirs, mine, query, intra, update, tokens, w_out, attention, gated, resid, ffn_in):
    span, width = tokens.shape
    place = positions(span, HEAD)
    for h in range(HEADS):
        lanes = slice(h * HEAD, (h + 1) * HEAD)
        wide = slice(2 * h * HEAD, 2 * (h + 1) * HEAD)
        lead = jnp.exp(-forget[h] * (place + 1.0))
        attention[:, lanes] = intra[:, lanes] + dot_nn(query[:, wide], state_of(numbers, mine, theirs, h)) * lead
    whole = attention[...]
    low = (whole * norm_scale(whole) * update[...]).astype(BF)
    gated[...] = low
    after = tokens[...].astype(F32) + dot_nn(low, w_out[...])
    resid[...] = after
    ffn_in[...] = (after * norm_scale(after)).astype(BF)


def ffn_kernel(rows_0, rows_1, hidden_grad, w_gate, w_up, hidden, gate_grad, up_grad, back_0, back_1):
    span = rows_0.shape[0]
    for i, (rows, back) in enumerate(((rows_0, back_0), (rows_1, back_1))):
        block = slice(i * span, (i + 1) * span)
        gate_pre = dot_nt(rows[...], w_gate[...])
        up_pre = dot_nt(rows[...], w_up[...])
        hidden[block] = (gate_pre * up_pre).astype(BF)
        upstream = hidden_grad[block]
        gate_low = (upstream * up_pre).astype(BF)
        up_low = (upstream * gate_pre).astype(BF)
        gate_grad[block] = gate_low
        up_grad[block] = up_low
        back[...] = (dot_nn(gate_low, w_gate[...]) + dot_nn(up_low, w_up[...])).astype(BF)


def hidden_grad_kernel(rows_0, rows_1, rows_2, rows_3, w_down, near, far):
    span = rows_0.shape[0]
    for rows, target, block in (
        (rows_0, near, slice(0, span)),
        (rows_1, near, slice(span, 2 * span)),
        (rows_2, far, slice(0, span)),
        (rows_3, far, slice(span, 2 * span)),
    ):
        target[block] = dot_nt(rows[...], w_down[...])


def down_kernel(hidden_near, hidden_far, w_down, own, other, far, cross):
    span = own.shape[0]
    for source, target, block in (
        (hidden_near, own, slice(0, span)),
        (hidden_near, other, slice(span, 2 * span)),
        (hidden_far, far, slice(0, span)),
        (hidden_far, cross, slice(span, 2 * span)),
    ):
        target[...] = dot_nn(source[block], w_down[...]).astype(BF)


def add_kernel(first, second, total):
    total[...] = (first[...].astype(F32) + second[...].astype(F32)).astype(BF)


def out_kernel(numbers, lengths, part_0, part_1, part_2, resid, out):
    valid = valid_rows(numbers, lengths, resid.shape)
    down = part_0[...].astype(F32) + part_1[...].astype(F32) + part_2[...].astype(F32)
    out[...] = jnp.where(valid, resid[...] + down, 0.0).astype(BF)


def resid_kernel(
    forget, numbers, part_0, part_1, part_2, resid, down_low, attention, update, query, w_out,
    resid_grad, mix_grad, update_grad, attention_grad, send, keep,
):
    span, width = resid.shape
    ffn_grad = part_0[...].astype(F32) + part_1[...].astype(F32) + part_2[...].astype(F32)
    total = down_low[...].astype(F32) + norm_back(resid[...], ffn_grad)
    resid_grad[...] = total
    low = total.astype(BF)
    mix_grad[...] = low
    gated_grad = dot_nt(low, w_out[...])
    whole = attention[...]
    r = norm_scale(whole)
    update_grad[...] = (gated_grad * (whole * r)).astype(BF)
    upstream = gated_grad * update[...]
    back = r * upstream - whole * (r * r * r * jnp.mean(whole * upstream, axis=-1, keepdims=True))
    attention_grad[...] = back.astype(BF)
    place = positions(span, HEAD)
    moments = []
    for h in range(HEADS):
        lanes = slice(h * HEAD, (h + 1) * HEAD)
        wide = slice(2 * h * HEAD, 2 * (h + 1) * HEAD)
        first = jnp.exp(-forget[h] * place)
        moments.append(dot_tn(query[:, wide], (attention_grad[:, lanes].astype(F32) * first).astype(BF)).astype(BF))
    low_side = numbers[0] == 0
    for h in range(HALF):
        keep[h] = jnp.where(low_side, moments[h], moments[h + HALF])
        send[h] = jnp.where(low_side, moments[h + HALF], moments[h])


def early_kernel(
    numbers, forget, grad, value, key, query, scores, theirs, mine, raw_query, cosine, sine, update_grad, mix_grad,
    piece_0, piece_1, piece_2, piece_3, key_part, value_part, pieces,
):
    span, width = update_grad.shape
    place = positions(span, 2 * HEAD)
    for h in range(HEADS):
        lanes = slice(h * HEAD, (h + 1) * HEAD)
        wide = slice(2 * h * HEAD, 2 * (h + 1) * HEAD)
        upstream = grad[:, lanes]
        low = (dot_nt(upstream, value[:, lanes]) * decay_grid(forget[h], span)).astype(BF)
        lead = jnp.exp(-forget[h] * (place + 1.0))
        query_grad = dot_nn(low, key[:, wide]) + dot_nt(upstream, state_of(numbers, mine, theirs, h)) * lead
        slope = slope_of(raw_query[:, lanes])
        start = (h % 2) * HEAD
        pieces[h // 2, :, start : start + HEAD] = (slope * fold(query_grad, cosine[...], sine[...])).astype(BF)
        key_part[:, lanes] = fold(dot_tn(low, query[:, wide]), cosine[...], sine[...])
        value_part[:, lanes] = dot_tn(scores[h], upstream)
    for j in range(width // PAIR):
        columns = slice(j * PAIR, (j + 1) * PAIR)
        pieces[j, :, PAIR : 2 * PAIR] = update_grad[:, columns]
        pieces[j, :, 2 * PAIR :] = mix_grad[:, columns]
    for k, piece in enumerate((piece_0, piece_1, piece_2, piece_3)):
        piece[...] = pieces[numbers[2] ^ k]


def late_kernel(
    numbers, forget, theirs, mine, value, key, raw_key, cosine, sine, key_part, value_part,
    piece_0, piece_1, piece_2, piece_3, pieces,
):
    span, width = value.shape
    place = positions(span, HEAD)
    for h in range(HEADS):
        lanes = slice(h * HEAD, (h + 1) * HEAD)
        wide = slice(2 * h * HEAD, 2 * (h + 1) * HEAD)
        after = state_of(numbers, mine, theirs, h)
        rear = jnp.exp(-forget[h] * (span - place))
        key_grad = fold(dot_nt(value[:, lanes], after), cosine[...], sine[...]) * rear + key_part[:, lanes]
        value_grad = dot_nn(key[:, wide], after) * rear + value_part[:, lanes]
        start = (h % 2) * HEAD
        pieces[h // 2, :, start : start + HEAD] = (slope_of(raw_key[:, lanes]) * key_grad).astype(BF)
        pieces[h // 2, :, PAIR + start : PAIR + start + HEAD] = value_grad.astype(BF)
    for k, piece in enumerate((piece_0, piece_1, piece_2, piece_3)):
        piece[...] = pieces[numbers[2] ^ k]


BITS = {"y": 1, "z1": 2, "z2": 4}


def bit_of(numbers, name):
    return numbers[0] if name == "y" else numbers[1] % 2 if name == "z1" else numbers[1] // 2


def split_blocks(order, numbers, keep, send, parts, index):
    mine = bit_of(numbers, order[0]) == 0
    for place in range(4):
        rest = BITS[order[1]] * (place // 2) + BITS[order[2]] * (place % 2)
        zero, one = parts[rest], parts[rest + BITS[order[0]]]
        keep[(place, *index)] = jnp.where(mine, zero, one)
        send[(place, *index)] = jnp.where(mine, one, zero)


def mix_weight_kernel(groups, order, numbers, *refs):
    inputs, send, keep = refs[:-2], refs[-2], refs[-1]
    part = keep.shape[1]
    start = 0
    for left, right, low, high in groups:
        total = None
        for a, b in zip(left, right):
            term = dot_tn(inputs[a][...], inputs[b][:, low:high])
            total = term if total is None else total + term
        parts = [total[m * part : (m + 1) * part].astype(BF) for m in range(8)]
        split_blocks(order, numbers, keep, send, parts, (slice(None), slice(start, start + high - low)))
        start += high - low


def ffn_weight_kernel(order, numbers, *refs):
    near, far, rows, send, keep = refs[0], refs[1], refs[2:6], refs[-2], refs[-1]
    span = rows[0].shape[0]
    units = near.shape[1]
    part = keep.shape[2]
    step = 256
    for low in range(0, units, step):
        high = min(low + step, units)
        total = None
        for i in range(4):
            source = near if i < 2 else far
            term = dot_tn(source[(i % 2) * span : (i % 2 + 1) * span, low:high], rows[i][...])
            total = term if total is None else total + term
        parts = [total[:, m * part : (m + 1) * part].astype(BF) for m in range(8)]
        split_blocks(order, numbers, keep, send, parts, (slice(low, high), slice(None)))


def whole_mix_weight_kernel(groups, numbers, *refs):
    inputs, target = refs[:-1], refs[-1]
    start = 0
    for left, right, low, high in groups:
        total = None
        for a, b in zip(left, right):
            term = dot_tn(inputs[a][...], inputs[b][:, low:high])
            total = term if total is None else total + term
        target[:, start : start + high - low] = total.astype(BF)
        start += high - low


def whole_ffn_weight_kernel(numbers, *refs):
    near, far, rows, target = refs[0], refs[1], refs[2:6], refs[-1]
    span = rows[0].shape[0]
    total = None
    for i in range(4):
        source = near if i < 2 else far
        term = dot_tn(source[(i % 2) * span : (i % 2 + 1) * span], rows[i][...])
        total = term if total is None else total + term
    target[...] = total.astype(BF)


def join_kernel(name, numbers, other, keep, send, own):
    mine = bit_of(numbers, name)
    count = own.shape[0]
    for i in range(count):
        for target, half in ((own, mine), (send, 1 - mine)):
            total = keep[half * count + i].astype(F32) + other[half * count + i].astype(F32)
            target[i] = total.astype(target.dtype)


def sum_kernel(other, keep, total):
    total[...] = (keep[0].astype(F32) + other[0].astype(F32)).astype(total.dtype)


class Reduction:
    def __init__(self, line, name, numbers, order, blocks_first, kernel, whole_kernel, shape, arrays, time):
        self.line, self.name, self.numbers, self.order = line, name, numbers, order
        self.fast = lax.axis_size("seq") == 8
        self.blocks_first = blocks_first
        if self.fast:
            rows, columns = shape
            block = (rows // 8, columns) if blocks_first else (rows, columns // 8)
            outs = [((4, *block), BF)] * 2
            self.send, self.keep = line.run(name, partial(kernel, order), outs, [numbers], arrays, time)
        else:
            self.whole = line.run(name, whole_kernel, [(shape, BF)], [numbers], arrays, time)[0]
        self.step = 0
        if not self.fast:
            self.send = self.whole

    def go(self):
        if self.fast:
            self.other = self.line.swap(self.send, "seq", BITS[self.order[self.step]])

    def wait(self):
        if self.fast:
            self.line.wait(self.other)

    def join(self):
        self.step += 1
        if self.fast:
            count, *block = self.keep.shape
            kind = F32 if count == 2 else BF
            self.send, self.keep = self.line.run(
                f"{self.name}_join{self.step}",
                partial(join_kernel, self.order[self.step]),
                [((count // 2, *block), BF), ((count // 2, *block), kind)],
                [self.numbers],
                [self.other, self.keep],
            )

    def total(self, kind):
        if self.fast:
            block = self.keep.shape[1:]
            return self.line.run(self.name + "_sum", sum_kernel, [(block, kind)], [], [self.other, self.keep])[0]
        return lax.psum_scatter(
            self.whole, "seq", scatter_dimension=0 if self.blocks_first else 1, tiled=True
        ).astype(kind)


def normed_grad_kernel(pieces, w_mix, target):
    total = None
    count = pieces.shape[0]
    for j in range(count):
        for source, block in ((0, 0), (1, 3)):
            term = dot_nt(pieces[j, :, source * PAIR : (source + 1) * PAIR], columns_of(w_mix, block, j))
            total = term if total is None else total + term
    target[...] = total


def tokens_kernel(pieces, early, resid_grad, tokens, w_mix, target):
    total = early[...]
    count = pieces.shape[0]
    for j in range(count):
        for source, block in ((0, 1), (1, 2)):
            total = total + dot_nt(pieces[j, :, source * PAIR : (source + 1) * PAIR], columns_of(w_mix, block, j))
    target[...] = (resid_grad[...] + norm_back(tokens[...].astype(F32), total)).astype(BF)


def collect_kernel(numbers, *refs):
    early, late, mix, out = refs[1:5], (*refs[5:8], refs[0]), refs[8], refs[9]
    quarter = out.shape[1] // 4
    width = out.shape[1]
    owner = numbers[2]

    def pick(parts, j, block):
        columns = slice(block * quarter, (block + 1) * quarter)
        a, b, c, d = (parts[j ^ k][:, columns].astype(F32) for k in range(4))
        return jnp.where(owner < 2, jnp.where(owner == 0, a, b), jnp.where(owner == 2, c, d))

    for j in range(4):
        columns = lambda block: slice(block * width + j * quarter, block * width + (j + 1) * quarter)
        mix[:, columns(0)] = pick(early, j, 0)
        mix[:, columns(1)] = pick(late, j, 0)
        mix[:, columns(2)] = pick(late, j, 1)
        mix[:, columns(3)] = pick(early, j, 1)
        out[:, columns(0)] = pick(early, j, 2)


def on_device(tokens, lengths, forget, w_mix, w_out, w_gate, w_up, w_down, cotangent):
    shape = tokens.shape
    _, span, width = shape
    units = w_gate.shape[1]
    quarter = width // 4
    place = lax.axis_index("seq")
    owner = lax.axis_index("tp")
    numbers = jnp.stack([place % 2, place // 2, owner]).astype(jnp.int32)
    cosine, sine = rotation(place * span + jnp.arange(span, dtype=jnp.int32), HEAD)
    tokens = tokens.reshape(span, width)
    cotangent = cotangent.reshape(span, width)
    w_gate, w_up, w_down = w_gate.T, w_up.T, w_down.T
    small = (span, width)
    state = ((HALF, 2 * HEAD, HEAD), BF)
    line = Line()
    got = {}

    normed, raw_key, key, value, send, keep = line.run(
        "key_value",
        key_value_kernel,
        [(small, BF), (small, F32), ((span, 2 * width), BF), (small, BF), state, state],
        [numbers, forget],
        [tokens, cosine, sine, w_mix],
    )
    line.last = normed

    def fore_1(_):
        got["query"] = line.run(
            "query",
            query_kernel,
            [(small, F32), ((span, 2 * width), BF), (small, F32), ((HEADS, span, span), BF), (small, F32), (small, BF)],
            [numbers, lengths, forget],
            [normed, key, value, cosine, sine, w_mix, cotangent],
        )

    def fore_2(other):
        got["down_far"] = line.swap(got["query"][5], "tp", 2)

    def fore_3(near):
        got["normed_far"] = line.swap(normed, "tp", 2)
        got["down_near"] = line.swap(got["query"][5], "tp", 1)
        line.wait(got["down_far"], got["down_near"])

    def fore_4(far):
        got["down_cross"] = line.swap(got["down_far"], "tp", 1)
        line.wait(got["down_cross"], got["normed_far"])

    mine, theirs = scan(line, send, keep, numbers, forget, span, False, (fore_1, fore_2, fore_3, fore_4))
    raw_query, query, update, scores, intra, down_low = got["query"]
    down_rows = [down_low, got["down_near"], got["down_far"], got["down_cross"]]

    attention, gated, resid, ffn_in = line.run(
        "mix",
        mix_kernel,
        [(small, F32), (small, BF), (small, F32), (small, BF)],
        [numbers, forget],
        [theirs, mine, query, intra, update, tokens, w_out],
    )
    ffn_rows = [ffn_in, line.swap(ffn_in, "tp", 1), line.swap(ffn_in, "tp", 2)]
    normed_rows = [normed, line.swap(normed, "tp", 1), got["normed_far"], line.swap(got["normed_far"], "tp", 1)]
    gated_near = line.swap(gated, "tp", 1)
    hidden_grad = line.run(
        "hidden_grad", hidden_grad_kernel, [((2 * span, units), F32)] * 2, [], [*down_rows, w_down],
    )

    def ffn(name, first, second, upstream):
        return line.run(
            name,
            lambda rows_1, rows_0, *rest: ffn_kernel(rows_0, rows_1, *rest),
            [((2 * span, units), BF)] * 3 + [(small, BF)] * 2,
            [],
            [second, first, upstream, w_gate, w_up],
        )

    line.wait(normed_rows[1], normed_rows[3], gated_near)
    hidden_near, gate_near, up_near, back_0, back_1 = ffn("ffn_near", ffn_rows[0], ffn_rows[1], hidden_grad[0])
    ffn_rows.append(line.swap(ffn_rows[2], "tp", 1))
    hidden_far, gate_far, up_far, back_2, back_3 = ffn("ffn_far", ffn_rows[2], ffn_rows[3], hidden_grad[1])
    part_1, from_3 = line.swap(back_1, "tp", 1), line.swap(back_3, "tp", 1)

    def ffn_weight(name, order, near, far, rows, time=BRIEF):
        return Reduction(
            line, name, numbers, order, False, ffn_weight_kernel, whole_ffn_weight_kernel, (units, width),
            [near, far, *rows], time,
        )

    y_first, z_first = ("y", "z1", "z2"), ("z1", "y", "z2")
    gate_sum = ffn_weight("d_gate", y_first, gate_near, gate_far, ffn_rows)
    gate_sum.go()
    line.wait(part_1)
    part_2 = line.run("ffn_add", add_kernel, [(small, BF)], [], [from_3, back_2])[0]
    part_2 = line.swap(part_2, "tp", 2)
    down_sum = ffn_weight("d_down", z_first, hidden_near, hidden_far, down_rows)
    down_sum.go()
    downs = line.run(
        "down", down_kernel, [(small, BF)] * 4, [], [hidden_near, hidden_far, w_down],
    )
    down_1, down_3 = line.swap(downs[1], "tp", 1), line.swap(downs[3], "tp", 1)
    up_sum = ffn_weight("d_up", y_first, up_near, up_far, ffn_rows)
    resid_grad, mix_grad, update_grad, attention_grad, send, keep = line.run(
        "resid",
        resid_kernel,
        [(small, F32), (small, BF), (small, BF), (small, BF), state, state],
        [forget, numbers],
        [part_2, back_0, part_1, resid, down_low, attention, update, query, w_out],
    )

    def mix_weight(name, groups, arrays, columns, time=BRIEF):
        return Reduction(
            line, name, numbers, y_first, True,
            lambda order, *refs: mix_weight_kernel(groups, order, *refs),
            partial(whole_mix_weight_kernel, groups),
            (width, columns), arrays, time,
        )

    four, more, most = (0, 1, 2, 3), (4, 5, 6, 7), (8, 9, 10, 11)

    def back_1_(_):
        got["gated_far"] = line.swap(gated, "tp", 2)
        gate_sum.wait()
        line.wait(down_1, down_3)
        got["early"] = line.run(
            "early",
            early_kernel,
            [((span, 3 * quarter), BF)] * 4 + [(small, F32)] * 2 + [((4, span, 3 * quarter), BF)],
            [numbers, forget],
            [attention_grad, value, key, query, scores, theirs, mine, raw_query, cosine, sine, update_grad, mix_grad],
        )
        got["early_2"], got["early_3"] = line.swap(got["early"][2], "tp", 2), line.swap(got["early"][3], "tp", 3)
        got["down_2"] = line.run("down_add", add_kernel, [(small, BF)], [], [down_3, downs[2]])[0]
        down_sum.wait()

    def back_2_(other):
        up_sum.go()
        line.wait(got["gated_far"])

    def back_3_(near):
        got["gated_cross"] = line.swap(got["gated_far"], "tp", 1)
        up_sum.wait()
        line.wait(got["early_2"], got["early_3"], got["gated_cross"])

    def back_4_(far):
        got["early_1"] = line.swap(got["early"][1], "tp", 1)
        gate_sum.join()
        gate_sum.go()
        up_sum.join()
        up_sum.go()
        down_sum.join()
        got["normed_grad"] = line.run(
            "normed_grad", normed_grad_kernel, [(small, F32)], [], [got["early"][6], w_mix],
        )[0]
        got["early_sum"] = mix_weight(
            "d_early",
            [(most, four, 0, 2 * quarter), (more, four, 2 * quarter, 3 * quarter)],
            [got["early_1"], got["early"][0], got["early_2"], got["early_3"]]
            + [gated_near, gated, got["gated_far"], got["gated_cross"]]
            + [normed_rows[k] for k in (1, 0, 2, 3)],
            3 * quarter,
        )

    after_mine, after_theirs = scan(
        line, send, keep, numbers, forget, span, True, (back_1_, back_2_, back_3_, back_4_)
    )
    key_part, value_part = got["early"][4:6]
    early_sum = got["early_sum"]
    *late, late_pieces = line.run(
        "late",
        late_kernel,
        [((span, 2 * quarter), BF)] * 4 + [((4, span, 2 * quarter), BF)],
        [numbers, forget],
        [after_theirs, after_mine, value, key, raw_key, cosine, sine, key_part, value_part],
    )
    late_2, late_3 = line.swap(late[2], "tp", 2), line.swap(late[3], "tp", 3)
    late_1 = line.swap(late[1], "tp", 1)
    down_sum.go()
    early_sum.go()
    gate_sum.join()
    gate_sum.go()
    line.wait(late_2, late_3)
    late_sum = mix_weight(
        "d_late",
        [(more, four, 0, 2 * quarter)],
        [late_1, late[0], late_2, late_3] + [normed_rows[k] for k in (1, 0, 2, 3)],
        2 * quarter,
    )
    late_sum.go()
    up_sum.join()
    up_sum.go()
    down_2 = line.swap(got["down_2"], "tp", 2)
    gate_grad = gate_sum.total(F32)
    down_sum.join()
    down_sum.go()
    d_tokens = line.run(
        "d_tokens",
        tokens_kernel,
        [(small, BF)],
        [],
        [late_pieces, got["normed_grad"], resid_grad, tokens, w_mix],
    )[0]
    up_grad = up_sum.total(F32)
    early_sum.join()
    early_sum.go()
    out = line.run("out", out_kernel, [(small, BF)], [numbers, lengths], [down_2, downs[0], down_1, resid])[0]
    down_grad = down_sum.total(F32)
    early_sum.join()
    early_sum.go()
    late_sum.join()
    late_sum.go()
    early_all = early_sum.total(BF)
    early_full = [early_all, line.swap(early_all, "tp", 1), line.swap(early_all, "tp", 2)]
    late_sum.join()
    late_sum.go()
    late_all = late_sum.total(BF)
    early_full.append(line.swap(early_full[2], "tp", 1))
    late_full = [late_all, line.swap(late_all, "tp", 1), line.swap(late_all, "tp", 2)]
    late_full.append(swap(late_full[2], "tp", 1))
    rows = early_full[0].shape[0]
    mix_sum, out_sum = line.run(
        "collect",
        collect_kernel,
        [((rows, 4 * width), F32), ((rows, width), F32)],
        [numbers],
        [late_full[3], *early_full, *late_full[:3]],
    )
    return (out.reshape(shape), d_tokens.reshape(shape), mix_sum, out_sum, gate_grad.T, up_grad.T, down_grad.T)


def solution(mesh):
    in_specs = (
        P("tp", "seq", None),
        P(),
        P(),
        P(),
        P(),
        P(None, "tp"),
        P(None, "tp"),
        P(None, "tp"),
        P("tp", "seq", None),
    )
    out_specs = (
        P("tp", "seq", None),
        P("tp", "seq", None),
        P("seq", None),
        P("seq", None),
        P("seq", "tp"),
        P("seq", "tp"),
        P("seq", "tp"),
    )
    return jax.shard_map(
        on_device, mesh=mesh, in_specs=in_specs, out_specs=out_specs, check_vma=False
    )
```

```python
from functools import partial
import math

import jax
import jax.numpy as jnp
import numpy as np
from jax import lax
from jax.experimental import pallas as pl
from jax.experimental.pallas import tpu as pltpu
from jax.sharding import PartitionSpec as P

HEADS = 8
HEAD = 128
HALF = HEADS // 2
PAIR = 2 * HEAD
EPSILON = 1e-06
BF = jnp.bfloat16
F32 = jnp.float32
SMALL = pl.BlockSpec(memory_space=pltpu.SMEM)
WHOLE = pl.BlockSpec(memory_space=pltpu.VMEM)
MIB = 1024 * 1024
ROOM = 4
BRIEF = 0.02
LONG = 6.0


def norm_scale(value):
    return lax.rsqrt(jnp.mean(value * value, axis=-1, keepdims=True) + EPSILON)


def norm_back(value, upstream):
    r = norm_scale(value)
    return r * upstream - value * (r * r * r * jnp.mean(value * upstream, axis=-1, keepdims=True))


def dot_nn(left, right):
    return jnp.dot(left, right, preferred_element_type=F32)


def dot_nt(left, right):
    return lax.dot_general(left, right, (((1,), (1,)), ((), ())), preferred_element_type=F32)


def dot_tn(left, right):
    return lax.dot_general(left, right, (((0,), (0,)), ((), ())), preferred_element_type=F32)


def rotation(places, width):
    table = np.floor(
        65536.0 / (2.0 * math.pi) * 10000.0 ** (-np.arange(width) / width) + 0.5
    ).astype(np.int32)
    phase = jnp.remainder(places[:, None] * jnp.asarray(table)[None, :], 65536)
    angle = phase.astype(F32) * (2.0 * math.pi / 65536.0)
    return (jnp.cos(angle), jnp.sin(angle))


def swap(array, axis, bit):
    count = lax.axis_size(axis)
    return lax.ppermute(array, axis, [(i, i ^ bit) for i in range(count)])


def tie(array, *others):
    return lax.optimization_barrier((array, *others))[0]


def positions(rows, columns):
    return lax.broadcasted_iota(jnp.int32, (rows, columns), 0).astype(F32)


def decay_grid(rate, span):
    gap = positions(span, span) - lax.broadcasted_iota(jnp.int32, (span, span), 1).astype(F32)
    return jnp.where(gap >= 0, jnp.exp(-rate * jnp.maximum(gap, 0.0)), 0.0)


def spread(values, cosine, sine):
    return jnp.concatenate([values * cosine, values * sine], axis=1).astype(BF)


def fold(grad, cosine, sine):
    return grad[:, :HEAD] * cosine + grad[:, HEAD:] * sine


def slope_of(raw):
    gate = jax.nn.sigmoid(raw)
    return gate * (1.0 + raw * (1.0 - gate))


def shape_of(shape, kind):
    return jax.ShapeDtypeStruct(shape, kind)


def params(room):
    return pltpu.CompilerParams(vmem_limit_bytes=int(room))


def cost(span_us):
    return pl.CostEstimate(flops=int(span_us * 1.1e9), bytes_accessed=1024, transcendentals=0)


class Line:
    def __init__(self):
        self.last = None
        self.more = []

    def wait(self, *arrays):
        self.more += arrays

    def hold(self, array):
        return array if self.last is None else tie(array, self.last)

    def swap(self, array, axis, bit):
        return swap(self.hold(array), axis, bit)

    def run(self, name, kernel, outs, scalars, arrays, time=BRIEF):
        arrays = list(arrays)
        arrays[0] = self.hold(arrays[0])
        if self.more:
            arrays[0] = tie(arrays[0], *self.more)
            self.more = []
        moved = sum(a.size * a.dtype.itemsize for a in arrays)
        moved += sum(math.prod(s) * jnp.dtype(k).itemsize for s, k in outs)
        results = pl.pallas_call(
            kernel,
            name=name,
            out_shape=[shape_of(s, k) for s, k in outs],
            in_specs=[SMALL] * len(scalars) + [WHOLE] * len(arrays),
            out_specs=[WHOLE] * len(outs),
            compiler_params=params(moved * 1.125 + ROOM * MIB),
            cost_estimate=cost(time),
        )(*scalars, *arrays)
        self.last = results[0]
        return results


def left_of(numbers, lengths, span):
    return lengths[numbers[2]] - (2 * numbers[1] + numbers[0]) * span


def valid_rows(numbers, lengths, shape):
    return lax.broadcasted_iota(jnp.int32, shape, 0) < left_of(numbers, lengths, shape[0])


def columns_of(w_mix, block, j):
    groups = w_mix.shape[1] // (4 * PAIR)
    return w_mix[:, (block * groups + j) * PAIR : (block * groups + j + 1) * PAIR]


def key_value_kernel(numbers, forget, tokens, cosine, sine, w_mix, normed, raw_key, key, value, send, keep):
    span, width = tokens.shape
    groups = width // PAIR
    inputs = tokens[...].astype(F32)
    rows = (inputs * norm_scale(inputs)).astype(BF)
    normed[...] = rows
    place = positions(span, HEAD)
    states = []
    for g in range(groups):
        lanes = slice(g * PAIR, (g + 1) * PAIR)
        raw = dot_nn(rows, columns_of(w_mix, 1, g))
        raw_key[:, lanes] = raw
        low = dot_nn(rows, columns_of(w_mix, 2, g)).astype(BF)
        value[:, lanes] = low
        active = raw * jax.nn.sigmoid(raw)
        for h in range(2):
            part = slice(h * HEAD, (h + 1) * HEAD)
            turned = spread(active[:, part], cosine[...], sine[...])
            start = 2 * (2 * g + h) * HEAD
            key[:, start : start + 2 * HEAD] = turned
            tail = jnp.exp(-forget[2 * g + h] * (span - 1.0 - place))
            states.append(dot_tn(turned, (low[:, part].astype(F32) * tail).astype(BF)).astype(BF))
    low_side = numbers[0] == 0
    for h in range(HALF):
        keep[h] = jnp.where(low_side, states[h], states[h + HALF])
        send[h] = jnp.where(low_side, states[h + HALF], states[h])


def query_kernel(
    numbers, lengths, forget, normed, key, value, cosine, sine, w_mix, cotangent,
    raw_query, query, update, scores, intra, down_low,
):
    span, width = normed.shape
    upstream = cotangent[...]
    down_low[...] = jnp.where(valid_rows(numbers, lengths, upstream.shape), upstream, jnp.zeros_like(upstream))
    groups = width // PAIR
    rows = normed[...]
    for g in range(groups):
        lanes = slice(g * PAIR, (g + 1) * PAIR)
        raw = dot_nn(rows, columns_of(w_mix, 0, g))
        raw_query[:, lanes] = raw
        update[:, lanes] = dot_nn(rows, columns_of(w_mix, 3, g))
        active = raw * jax.nn.sigmoid(raw)
        for h in range(2):
            head = 2 * g + h
            part = slice(head * HEAD, (head + 1) * HEAD)
            wide = slice(2 * head * HEAD, 2 * (head + 1) * HEAD)
            turned = spread(active[:, h * HEAD : (h + 1) * HEAD], cosine[...], sine[...])
            query[:, wide] = turned
            low = (dot_nt(turned, key[:, wide]) * decay_grid(forget[head], span)).astype(BF)
            scores[head] = low
            intra[:, part] = dot_nn(low, value[:, part])


def stand(numbers, backward):
    side, layer = numbers[0], numbers[1]
    low = side == 1 if backward else side == 0
    depth = 3 - layer if backward else layer
    return side, low, lax.rem(depth, 2) == 0, depth < 2


def block_rate(forget, side, h, span):
    return jnp.exp(jnp.zeros((1, HEAD), F32) - forget[side * HALF + h] * span)


def pair_kernel(backward, span, numbers, forget, keep, other, pair):
    side, low, _, _ = stand(numbers, backward)
    for h in range(HALF):
        rate = block_rate(forget, side, h, span)
        mine, theirs = keep[h].astype(F32), other[h].astype(F32)
        pair[h] = (jnp.where(low, rate, 1.0) * mine + jnp.where(low, 1.0, rate) * theirs).astype(BF)


def quad_kernel(backward, span, numbers, forget, pair, near, quad):
    side, _, even, _ = stand(numbers, backward)
    for h in range(HALF):
        rate = block_rate(forget, side, h, 2.0 * span)
        mine, theirs = pair[h].astype(F32), near[h].astype(F32)
        quad[h] = (jnp.where(even, rate, 1.0) * mine + jnp.where(even, 1.0, rate) * theirs).astype(BF)


def enter_kernel(backward, span, numbers, forget, near, far, keep, other, theirs, mine):
    side, low, even, early = stand(numbers, backward)
    for h in range(HALF):
        rate = block_rate(forget, side, h, span)
        double = block_rate(forget, side, h, 2.0 * span)
        from_near = jnp.where(even, 0.0, 1.0)
        from_far = jnp.where(early, 0.0, jnp.where(even, 1.0, double))
        before = from_near * near[h].astype(F32) + from_far * far[h].astype(F32)
        added = before * rate + jnp.where(low, keep[h].astype(F32), other[h].astype(F32))
        theirs[h] = jnp.where(low, added, before).astype(BF)
        mine[h] = jnp.where(low, before, added).astype(BF)


def scan_states(line, send, keep, numbers, forget, span, backward, fillers):
    name = "back" if backward else "fore"
    state = [(keep.shape, BF)]
    other = swap(send, "seq", 1)
    fillers[0](None)
    pair = line.run(name + "_pair", partial(pair_kernel, backward, span), state, [numbers, forget], [keep, other])[0]
    near = swap(pair, "seq", 2)
    fillers[1](other)
    quad = line.run(name + "_quad", partial(quad_kernel, backward, span), state, [numbers, forget], [pair, near])[0]
    far = swap(quad, "seq", 4)
    fillers[2](near)
    theirs, mine = line.run(
        name + "_enter", partial(enter_kernel, backward, span), state * 2, [numbers, forget], [near, far, keep, other]
    )
    theirs = swap(theirs, "seq", 1)
    fillers[3](far)
    return mine, theirs


def scan_any(state, forget, span, backward):
    count = lax.axis_size("seq")
    place = lax.axis_index("seq")
    ahead = count - 1 - place if backward else place
    carried = jnp.exp(-forget * span)[:, None, None]
    gathered = lax.all_gather(state, "seq")

    def one(hop, total):
        source = count - 1 - hop if backward else hop
        return total * carried + lax.dynamic_index_in_dim(gathered, source, 0, False).astype(F32)

    return lax.fori_loop(0, ahead, one, jnp.zeros(state.shape, F32)).astype(BF)


def by_side(side, mine, theirs):
    low = side == 0
    return jnp.where(low, jnp.concatenate([mine, theirs]), jnp.concatenate([theirs, mine]))


def scan(line, send, keep, numbers, forget, span, backward, fillers):
    if lax.axis_size("seq") == 8:
        return scan_states(line, send, keep, numbers, forget, span, backward, fillers)
    for filler in fillers:
        filler(None)
    whole = scan_any(by_side(numbers[0], keep, send), forget, span, backward)
    upper = numbers[0] == 0
    return jnp.where(upper, whole[:HALF], whole[HALF:]), jnp.where(upper, whole[HALF:], whole[:HALF])


def state_of(numbers, mine, theirs, h):
    first, second = (mine, theirs) if h < HALF else (theirs, mine)
    return jnp.where(numbers[0] == 0, first[h % HALF], second[h % HALF])


def mix_kernel(numbers, forget, theirs, mine, query, intra, update, tokens, w_out, attention, gated, resid, ffn_in):
    span, width = tokens.shape
    place = positions(span, HEAD)
    for h in range(HEADS):
        lanes = slice(h * HEAD, (h + 1) * HEAD)
        wide = slice(2 * h * HEAD, 2 * (h + 1) * HEAD)
        lead = jnp.exp(-forget[h] * (place + 1.0))
        attention[:, lanes] = intra[:, lanes] + dot_nn(query[:, wide], state_of(numbers, mine, theirs, h)) * lead
    whole = attention[...]
    low = (whole * norm_scale(whole) * update[...]).astype(BF)
    gated[...] = low
    after = tokens[...].astype(F32) + dot_nn(low, w_out[...])
    resid[...] = after
    ffn_in[...] = (after * norm_scale(after)).astype(BF)


def ffn_kernel(rows_0, rows_1, hidden_grad, w_gate, w_up, hidden, gate_grad, up_grad, back_0, back_1):
    span = rows_0.shape[0]
    for i, (rows, back) in enumerate(((rows_0, back_0), (rows_1, back_1))):
        block = slice(i * span, (i + 1) * span)
        gate_pre = dot_nt(rows[...], w_gate[...])
        up_pre = dot_nt(rows[...], w_up[...])
        hidden[block] = (gate_pre * up_pre).astype(BF)
        upstream = hidden_grad[block]
        gate_low = (upstream * up_pre).astype(BF)
        up_low = (upstream * gate_pre).astype(BF)
        gate_grad[block] = gate_low
        up_grad[block] = up_low
        back[...] = (dot_nn(gate_low, w_gate[...]) + dot_nn(up_low, w_up[...])).astype(BF)


def hidden_grad_kernel(rows_0, rows_1, rows_2, rows_3, w_down, near, far):
    span = rows_0.shape[0]
    for rows, target, block in (
        (rows_0, near, slice(0, span)),
        (rows_1, near, slice(span, 2 * span)),
        (rows_2, far, slice(0, span)),
        (rows_3, far, slice(span, 2 * span)),
    ):
        target[block] = dot_nt(rows[...], w_down[...])


def down_kernel(hidden_near, hidden_far, w_down, own, other, far, cross):
    span = own.shape[0]
    for source, target, block in (
        (hidden_near, own, slice(0, span)),
        (hidden_near, other, slice(span, 2 * span)),
        (hidden_far, far, slice(0, span)),
        (hidden_far, cross, slice(span, 2 * span)),
    ):
        target[...] = dot_nn(source[block], w_down[...]).astype(BF)


def add_kernel(first, second, total):
    total[...] = (first[...].astype(F32) + second[...].astype(F32)).astype(BF)


def out_kernel(numbers, lengths, part_0, part_1, part_2, resid, out):
    valid = valid_rows(numbers, lengths, resid.shape)
    down = part_0[...].astype(F32) + part_1[...].astype(F32) + part_2[...].astype(F32)
    out[...] = jnp.where(valid, resid[...] + down, 0.0).astype(BF)


def resid_kernel(
    forget, numbers, part_0, part_1, part_2, resid, down_low, attention, update, query, w_out,
    resid_grad, mix_grad, update_grad, attention_grad, send, keep,
):
    span, width = resid.shape
    ffn_grad = part_0[...].astype(F32) + part_1[...].astype(F32) + part_2[...].astype(F32)
    total = down_low[...].astype(F32) + norm_back(resid[...], ffn_grad)
    resid_grad[...] = total
    low = total.astype(BF)
    mix_grad[...] = low
    gated_grad = dot_nt(low, w_out[...])
    whole = attention[...]
    r = norm_scale(whole)
    update_grad[...] = (gated_grad * (whole * r)).astype(BF)
    upstream = gated_grad * update[...]
    back = r * upstream - whole * (r * r * r * jnp.mean(whole * upstream, axis=-1, keepdims=True))
    attention_grad[...] = back.astype(BF)
    place = positions(span, HEAD)
    moments = []
    for h in range(HEADS):
        lanes = slice(h * HEAD, (h + 1) * HEAD)
        wide = slice(2 * h * HEAD, 2 * (h + 1) * HEAD)
        first = jnp.exp(-forget[h] * place)
        moments.append(dot_tn(query[:, wide], (attention_grad[:, lanes].astype(F32) * first).astype(BF)).astype(BF))
    low_side = numbers[0] == 0
    for h in range(HALF):
        keep[h] = jnp.where(low_side, moments[h], moments[h + HALF])
        send[h] = jnp.where(low_side, moments[h + HALF], moments[h])


def early_kernel(
    numbers, forget, grad, value, key, query, scores, theirs, mine, raw_query, cosine, sine, update_grad, mix_grad,
    piece_0, piece_1, piece_2, piece_3, key_part, value_part, pieces,
):
    span, width = update_grad.shape
    place = positions(span, 2 * HEAD)
    for h in range(HEADS):
        lanes = slice(h * HEAD, (h + 1) * HEAD)
        wide = slice(2 * h * HEAD, 2 * (h + 1) * HEAD)
        upstream = grad[:, lanes]
        low = (dot_nt(upstream, value[:, lanes]) * decay_grid(forget[h], span)).astype(BF)
        lead = jnp.exp(-forget[h] * (place + 1.0))
        query_grad = dot_nn(low, key[:, wide]) + dot_nt(upstream, state_of(numbers, mine, theirs, h)) * lead
        slope = slope_of(raw_query[:, lanes])
        start = (h % 2) * HEAD
        pieces[h // 2, :, start : start + HEAD] = (slope * fold(query_grad, cosine[...], sine[...])).astype(BF)
        key_part[:, lanes] = fold(dot_tn(low, query[:, wide]), cosine[...], sine[...])
        value_part[:, lanes] = dot_tn(scores[h], upstream)
    for j in range(width // PAIR):
        columns = slice(j * PAIR, (j + 1) * PAIR)
        pieces[j, :, PAIR : 2 * PAIR] = update_grad[:, columns]
        pieces[j, :, 2 * PAIR :] = mix_grad[:, columns]
    for k, piece in enumerate((piece_0, piece_1, piece_2, piece_3)):
        piece[...] = pieces[numbers[2] ^ k]


def late_kernel(
    numbers, forget, theirs, mine, value, key, raw_key, cosine, sine, key_part, value_part,
    piece_0, piece_1, piece_2, piece_3, pieces,
):
    span, width = value.shape
    place = positions(span, HEAD)
    for h in range(HEADS):
        lanes = slice(h * HEAD, (h + 1) * HEAD)
        wide = slice(2 * h * HEAD, 2 * (h + 1) * HEAD)
        after = state_of(numbers, mine, theirs, h)
        rear = jnp.exp(-forget[h] * (span - place))
        key_grad = fold(dot_nt(value[:, lanes], after), cosine[...], sine[...]) * rear + key_part[:, lanes]
        value_grad = dot_nn(key[:, wide], after) * rear + value_part[:, lanes]
        start = (h % 2) * HEAD
        pieces[h // 2, :, start : start + HEAD] = (slope_of(raw_key[:, lanes]) * key_grad).astype(BF)
        pieces[h // 2, :, PAIR + start : PAIR + start + HEAD] = value_grad.astype(BF)
    for k, piece in enumerate((piece_0, piece_1, piece_2, piece_3)):
        piece[...] = pieces[numbers[2] ^ k]


BITS = {"y": 1, "z1": 2, "z2": 4}


def bit_of(numbers, name):
    return numbers[0] if name == "y" else numbers[1] % 2 if name == "z1" else numbers[1] // 2


def split_blocks(order, numbers, keep, send, parts, index):
    mine = bit_of(numbers, order[0]) == 0
    for place in range(4):
        rest = BITS[order[1]] * (place // 2) + BITS[order[2]] * (place % 2)
        zero, one = parts[rest], parts[rest + BITS[order[0]]]
        keep[(place, *index)] = jnp.where(mine, zero, one)
        send[(place, *index)] = jnp.where(mine, one, zero)


def mix_weight_kernel(groups, order, numbers, *refs):
    inputs, send, keep = refs[:-2], refs[-2], refs[-1]
    part = keep.shape[1]
    start = 0
    for left, right, low, high in groups:
        total = None
        for a, b in zip(left, right):
            term = dot_tn(inputs[a][...], inputs[b][:, low:high])
            total = term if total is None else total + term
        parts = [total[m * part : (m + 1) * part].astype(BF) for m in range(8)]
        split_blocks(order, numbers, keep, send, parts, (slice(None), slice(start, start + high - low)))
        start += high - low


def ffn_weight_kernel(order, numbers, *refs):
    near, far, rows, send, keep = refs[0], refs[1], refs[2:6], refs[-2], refs[-1]
    span = rows[0].shape[0]
    units = near.shape[1]
    part = keep.shape[2]
    step = 256
    for low in range(0, units, step):
        high = min(low + step, units)
        total = None
        for i in range(4):
            source = near if i < 2 else far
            term = dot_tn(source[(i % 2) * span : (i % 2 + 1) * span, low:high], rows[i][...])
            total = term if total is None else total + term
        parts = [total[:, m * part : (m + 1) * part].astype(BF) for m in range(8)]
        split_blocks(order, numbers, keep, send, parts, (slice(low, high), slice(None)))


def whole_mix_weight_kernel(groups, numbers, *refs):
    inputs, target = refs[:-1], refs[-1]
    start = 0
    for left, right, low, high in groups:
        total = None
        for a, b in zip(left, right):
            term = dot_tn(inputs[a][...], inputs[b][:, low:high])
            total = term if total is None else total + term
        target[:, start : start + high - low] = total.astype(BF)
        start += high - low


def whole_ffn_weight_kernel(numbers, *refs):
    near, far, rows, target = refs[0], refs[1], refs[2:6], refs[-1]
    span = rows[0].shape[0]
    total = None
    for i in range(4):
        source = near if i < 2 else far
        term = dot_tn(source[(i % 2) * span : (i % 2 + 1) * span], rows[i][...])
        total = term if total is None else total + term
    target[...] = total.astype(BF)


def join_kernel(name, numbers, other, keep, send, own):
    mine = bit_of(numbers, name)
    count = own.shape[0]
    for i in range(count):
        for target, half in ((own, mine), (send, 1 - mine)):
            total = keep[half * count + i].astype(F32) + other[half * count + i].astype(F32)
            target[i] = total.astype(target.dtype)


def sum_kernel(other, keep, total):
    total[...] = (keep[0].astype(F32) + other[0].astype(F32)).astype(total.dtype)


class Reduction:
    def __init__(self, line, name, numbers, order, blocks_first, kernel, whole_kernel, shape, arrays, time):
        self.line, self.name, self.numbers, self.order = line, name, numbers, order
        self.fast = lax.axis_size("seq") == 8
        self.blocks_first = blocks_first
        if self.fast:
            rows, columns = shape
            block = (rows // 8, columns) if blocks_first else (rows, columns // 8)
            outs = [((4, *block), BF)] * 2
            self.send, self.keep = line.run(name, partial(kernel, order), outs, [numbers], arrays, time)
        else:
            self.whole = line.run(name, whole_kernel, [(shape, BF)], [numbers], arrays, time)[0]
        self.step = 0
        if not self.fast:
            self.send = self.whole

    def go(self):
        if self.fast:
            self.other = self.line.swap(self.send, "seq", BITS[self.order[self.step]])

    def wait(self):
        if self.fast:
            self.line.wait(self.other)

    def join(self):
        self.step += 1
        if self.fast:
            count, *block = self.keep.shape
            kind = F32 if count == 2 else BF
            self.send, self.keep = self.line.run(
                f"{self.name}_join{self.step}",
                partial(join_kernel, self.order[self.step]),
                [((count // 2, *block), BF), ((count // 2, *block), kind)],
                [self.numbers],
                [self.other, self.keep],
            )

    def total(self, kind):
        if self.fast:
            block = self.keep.shape[1:]
            return self.line.run(self.name + "_sum", sum_kernel, [(block, kind)], [], [self.other, self.keep])[0]
        return lax.psum_scatter(
            self.whole, "seq", scatter_dimension=0 if self.blocks_first else 1, tiled=True
        ).astype(kind)


def normed_grad_kernel(pieces, w_mix, target):
    total = None
    count = pieces.shape[0]
    for j in range(count):
        for source, block in ((0, 0), (1, 3)):
            term = dot_nt(pieces[j, :, source * PAIR : (source + 1) * PAIR], columns_of(w_mix, block, j))
            total = term if total is None else total + term
    target[...] = total


def tokens_kernel(pieces, early, resid_grad, tokens, w_mix, target):
    total = early[...]
    count = pieces.shape[0]
    for j in range(count):
        for source, block in ((0, 1), (1, 2)):
            total = total + dot_nt(pieces[j, :, source * PAIR : (source + 1) * PAIR], columns_of(w_mix, block, j))
    target[...] = (resid_grad[...] + norm_back(tokens[...].astype(F32), total)).astype(BF)


def collect_kernel(numbers, *refs):
    early, late, mix, out = refs[1:5], (*refs[5:8], refs[0]), refs[8], refs[9]
    quarter = out.shape[1] // 4
    width = out.shape[1]
    owner = numbers[2]

    def pick(parts, j, block):
        columns = slice(block * quarter, (block + 1) * quarter)
        a, b, c, d = (parts[j ^ k][:, columns].astype(F32) for k in range(4))
        return jnp.where(owner < 2, jnp.where(owner == 0, a, b), jnp.where(owner == 2, c, d))

    for j in range(4):
        columns = lambda block: slice(block * width + j * quarter, block * width + (j + 1) * quarter)
        mix[:, columns(0)] = pick(early, j, 0)
        mix[:, columns(1)] = pick(late, j, 0)
        mix[:, columns(2)] = pick(late, j, 1)
        mix[:, columns(3)] = pick(early, j, 1)
        out[:, columns(0)] = pick(early, j, 2)


def on_device(tokens, lengths, forget, w_mix, w_out, w_gate, w_up, w_down, cotangent):
    shape = tokens.shape
    _, span, width = shape
    units = w_gate.shape[1]
    quarter = width // 4
    place = lax.axis_index("seq")
    owner = lax.axis_index("tp")
    numbers = jnp.stack([place % 2, place // 2, owner]).astype(jnp.int32)
    cosine, sine = rotation(place * span + jnp.arange(span, dtype=jnp.int32), HEAD)
    tokens = tokens.reshape(span, width)
    cotangent = cotangent.reshape(span, width)
    w_gate, w_up, w_down = w_gate.T, w_up.T, w_down.T
    small = (span, width)
    state = ((HALF, 2 * HEAD, HEAD), BF)
    line = Line()
    got = {}

    normed, raw_key, key, value, send, keep = line.run(
        "key_value",
        key_value_kernel,
        [(small, BF), (small, F32), ((span, 2 * width), BF), (small, BF), state, state],
        [numbers, forget],
        [tokens, cosine, sine, w_mix],
    )
    line.last = normed

    def fore_1(_):
        got["query"] = line.run(
            "query",
            query_kernel,
            [(small, F32), ((span, 2 * width), BF), (small, F32), ((HEADS, span, span), BF), (small, F32), (small, BF)],
            [numbers, lengths, forget],
            [normed, key, value, cosine, sine, w_mix, cotangent],
        )

    def fore_2(other):
        got["down_far"] = line.swap(got["query"][5], "tp", 2)

    def fore_3(near):
        got["normed_far"] = line.swap(normed, "tp", 2)
        got["down_near"] = line.swap(got["query"][5], "tp", 1)
        line.wait(got["down_far"], got["down_near"])

    def fore_4(far):
        got["down_cross"] = line.swap(got["down_far"], "tp", 1)
        line.wait(got["down_cross"], got["normed_far"])

    mine, theirs = scan(line, send, keep, numbers, forget, span, False, (fore_1, fore_2, fore_3, fore_4))
    raw_query, query, update, scores, intra, down_low = got["query"]
    down_rows = [down_low, got["down_near"], got["down_far"], got["down_cross"]]

    attention, gated, resid, ffn_in = line.run(
        "mix",
        mix_kernel,
        [(small, F32), (small, BF), (small, F32), (small, BF)],
        [numbers, forget],
        [theirs, mine, query, intra, update, tokens, w_out],
    )
    ffn_rows = [ffn_in, line.swap(ffn_in, "tp", 1), line.swap(ffn_in, "tp", 2)]
    normed_rows = [normed, line.swap(normed, "tp", 1), got["normed_far"], line.swap(got["normed_far"], "tp", 1)]
    gated_near = line.swap(gated, "tp", 1)
    hidden_grad = line.run(
        "hidden_grad", hidden_grad_kernel, [((2 * span, units), F32)] * 2, [], [*down_rows, w_down],
    )

    def ffn(name, first, second, upstream):
        return line.run(
            name,
            lambda rows_1, rows_0, *rest: ffn_kernel(rows_0, rows_1, *rest),
            [((2 * span, units), BF)] * 3 + [(small, BF)] * 2,
            [],
            [second, first, upstream, w_gate, w_up],
        )

    line.wait(normed_rows[1], normed_rows[3], gated_near)
    hidden_near, gate_near, up_near, back_0, back_1 = ffn("ffn_near", ffn_rows[0], ffn_rows[1], hidden_grad[0])
    ffn_rows.append(line.swap(ffn_rows[2], "tp", 1))
    hidden_far, gate_far, up_far, back_2, back_3 = ffn("ffn_far", ffn_rows[2], ffn_rows[3], hidden_grad[1])
    part_1, from_3 = line.swap(back_1, "tp", 1), line.swap(back_3, "tp", 1)

    def ffn_weight(name, order, near, far, rows, time=BRIEF):
        return Reduction(
            line, name, numbers, order, False, ffn_weight_kernel, whole_ffn_weight_kernel, (units, width),
            [near, far, *rows], time,
        )

    y_first, z_first = ("y", "z1", "z2"), ("z1", "y", "z2")
    gate_sum = ffn_weight("d_gate", y_first, gate_near, gate_far, ffn_rows)
    gate_sum.go()
    line.wait(part_1)
    part_2 = line.run("ffn_add", add_kernel, [(small, BF)], [], [from_3, back_2])[0]
    part_2 = line.swap(part_2, "tp", 2)
    down_sum = ffn_weight("d_down", z_first, hidden_near, hidden_far, down_rows)
    down_sum.go()
    downs = line.run(
        "down", down_kernel, [(small, BF)] * 4, [], [hidden_near, hidden_far, w_down],
    )
    down_1, down_3 = line.swap(downs[1], "tp", 1), line.swap(downs[3], "tp", 1)
    up_sum = ffn_weight("d_up", y_first, up_near, up_far, ffn_rows)
    resid_grad, mix_grad, update_grad, attention_grad, send, keep = line.run(
        "resid",
        resid_kernel,
        [(small, F32), (small, BF), (small, BF), (small, BF), state, state],
        [forget, numbers],
        [part_2, back_0, part_1, resid, down_low, attention, update, query, w_out],
        BRIEF,
    )

    def mix_weight(name, groups, arrays, columns, time=BRIEF):
        return Reduction(
            line, name, numbers, y_first, True,
            lambda order, *refs: mix_weight_kernel(groups, order, *refs),
            partial(whole_mix_weight_kernel, groups),
            (width, columns), arrays, time,
        )

    four, more, most = (0, 1, 2, 3), (4, 5, 6, 7), (8, 9, 10, 11)

    def back_1_(_):
        got["gated_far"] = line.swap(gated, "tp", 2)
        gate_sum.wait()
        line.wait(down_1, down_3)
        got["early"] = line.run(
            "early",
            early_kernel,
            [((span, 3 * quarter), BF)] * 4 + [(small, F32)] * 2 + [((4, span, 3 * quarter), BF)],
            [numbers, forget],
            [attention_grad, value, key, query, scores, theirs, mine, raw_query, cosine, sine, update_grad, mix_grad],
        )
        got["early_2"], got["early_3"] = line.swap(got["early"][2], "tp", 2), line.swap(got["early"][3], "tp", 3)
        got["down_2"] = line.run("down_add", add_kernel, [(small, BF)], [], [down_3, downs[2]])[0]
        down_sum.wait()

    def back_2_(other):
        up_sum.go()
        line.wait(got["gated_far"])

    def back_3_(near):
        got["gated_cross"] = line.swap(got["gated_far"], "tp", 1)
        up_sum.wait()
        line.wait(got["early_2"], got["early_3"], got["gated_cross"])

    def back_4_(far):
        got["early_1"] = line.swap(got["early"][1], "tp", 1)
        gate_sum.join()
        gate_sum.go()
        up_sum.join()
        up_sum.go()
        down_sum.join()
        got["normed_grad"] = line.run(
            "normed_grad", normed_grad_kernel, [(small, F32)], [], [got["early"][6], w_mix],
        )[0]
        got["early_sum"] = mix_weight(
            "d_early",
            [(most, four, 0, 2 * quarter), (more, four, 2 * quarter, 3 * quarter)],
            [got["early_1"], got["early"][0], got["early_2"], got["early_3"]]
            + [gated_near, gated, got["gated_far"], got["gated_cross"]]
            + [normed_rows[k] for k in (1, 0, 2, 3)],
            3 * quarter,
        )

    after_mine, after_theirs = scan(
        line, send, keep, numbers, forget, span, True, (back_1_, back_2_, back_3_, back_4_)
    )
    key_part, value_part = got["early"][4:6]
    *late, late_pieces = line.run(
        "late",
        late_kernel,
        [((span, 2 * quarter), BF)] * 4 + [((4, span, 2 * quarter), BF)],
        [numbers, forget],
        [after_theirs, after_mine, value, key, raw_key, cosine, sine, key_part, value_part],
        BRIEF,
    )
    late_2, late_3 = line.swap(late[2], "tp", 2), line.swap(late[3], "tp", 3)
    late_1 = line.swap(late[1], "tp", 1)
    down_sum.go()
    got["early_sum"].go()
    gate_sum.join()
    gate_sum.go()
    line.wait(late_2, late_3)
    late_sum = mix_weight(
        "d_late",
        [(more, four, 0, 2 * quarter)],
        [late_1, late[0], late_2, late_3] + [normed_rows[k] for k in (1, 0, 2, 3)],
        2 * quarter,
        BRIEF,
    )
    late_sum.go()
    up_sum.join()
    up_sum.go()
    down_2 = line.swap(got["down_2"], "tp", 2)
    gate_grad = gate_sum.total(F32)
    down_sum.join()
    down_sum.go()
    up_grad = up_sum.total(F32)
    got["early_sum"].join()
    got["early_sum"].go()
    d_tokens = line.run(
        "d_tokens",
        tokens_kernel,
        [(small, BF)],
        [],
        [late_pieces, got["normed_grad"], resid_grad, tokens, w_mix],
        BRIEF,
    )[0]
    got["early_sum"].join()
    got["early_sum"].go()
    out = line.run("out", out_kernel, [(small, BF)], [numbers, lengths], [down_2, downs[0], down_1, resid])[0]
    down_grad = down_sum.total(F32)
    late_sum.join()
    late_sum.go()
    early_all = got["early_sum"].total(BF)
    early_full = [early_all, line.swap(early_all, "tp", 1), line.swap(early_all, "tp", 2)]
    late_sum.join()
    late_sum.go()
    late_all = late_sum.total(BF)
    late_full = [late_all, line.swap(late_all, "tp", 1), line.swap(late_all, "tp", 2)]
    early_full.append(line.swap(early_full[2], "tp", 1))
    late_full.append(swap(late_full[2], "tp", 1))
    rows = early_full[0].shape[0]
    mix_sum, out_sum = line.run(
        "collect",
        collect_kernel,
        [((rows, 4 * width), F32), ((rows, width), F32)],
        [numbers],
        [late_full[3], *early_full, *late_full[:3]],
    )
    return (out.reshape(shape), d_tokens.reshape(shape), mix_sum, out_sum, gate_grad.T, up_grad.T, down_grad.T)


def solution(mesh):
    in_specs = (
        P("tp", "seq", None),
        P(),
        P(),
        P(),
        P(),
        P(None, "tp"),
        P(None, "tp"),
        P(None, "tp"),
        P("tp", "seq", None),
    )
    out_specs = (
        P("tp", "seq", None),
        P("tp", "seq", None),
        P("seq", None),
        P("seq", None),
        P("seq", "tp"),
        P("seq", "tp"),
        P("seq", "tp"),
    )
    return jax.shard_map(
        on_device, mesh=mesh, in_specs=in_specs, out_specs=out_specs, check_vma=False
    )
```
